32 devices in a mesh: inp: 8 (over z, core), tm: 4 (over y, x).
Axes of the slice: x: 2, y: 2, z: 4, core: 2. Of those that a mesh axis runs over, the one named last changes fastest.
Arguments:
- samples: bfloat16 [256, 786432], P('inp', 'tm'), may hold values from -6 to 6
- tap_weights: float32 [4, 512], replicated, may hold values from -3 to 3
Outputs:
- visibilities: float32 [256, 2, 256, 256], P('tm', None, 'inp')
The draws below stay inside these ranges and needn't reach their ends.
All inputs are finite; a program needn't handle non-finite values.
Results may differ from the reference program's by a relative error of at most 0.00081.
Values may be sent and summed in bfloat16 or wider, within the bound.
A program may use at most 128 MiB of HBM per device.

```python
import math
import jax
import jax.numpy as jnp
from jax import lax

INPUTS = 256
FRAME = 512
TAPS = 4
S_DEV = 384
CHANNELS = 256
NSPEC = 1536
SAMPLES = 786432
N_TM = 4


def block_levels(stream_key, shape, cuts, smallest, largest):
    gain = 1.0
    for axis_at, shards_of in cuts:
        steps = jax.random.uniform(jax.random.fold_in(jax.random.fold_in(stream_key, 6), axis_at), (shards_of,), jnp.float32, smallest / len(cuts), largest / len(cuts))
        gain = gain * jnp.repeat(jnp.exp(steps), shape[axis_at] // shards_of).reshape((-1,) + (1,) * (len(shape) - 1 - axis_at))
    return gain


def noise(key, dims, deviation, most, pieces=(), kind=jnp.bfloat16):
    array = jax.random.normal(key, dims, jnp.float32) * deviation
    if len(pieces) > 0:
        array = block_levels(key, dims, pieces, -0.22, 0.18) * array
    return jnp.clip(array, min=-most, max=most).astype(kind)


def setup_inputs(seed: int = 0) -> dict:
    splits = jax.random.split(jax.random.key(seed), 3)
    samples = noise(splits[0], (INPUTS, SAMPLES), 1.0, 6.0, ((0, 8), (1, 4)))
    tap_weights = noise(splits[1], (TAPS, FRAME), 0.5, 3.0, (), jnp.float32)
    return dict(samples=samples, tap_weights=tap_weights)


def reference(samples, tap_weights):
    frames = samples.reshape(INPUTS, NSPEC, FRAME)
    index_n = jnp.arange(FRAME, dtype=jnp.int32)
    index_c = jnp.arange(CHANNELS, dtype=jnp.int32)
    phase = index_n[:, None] * index_c[None, :] % FRAME
    angle = phase.astype(jnp.float32) * (2.0 * math.pi / FRAME)
    table = jnp.concatenate([jnp.cos(angle), -jnp.sin(angle)], axis=1) * FRAME ** (-0.5)
    weights = tap_weights.astype(jnp.float32)

    def block(total, segment):
        start = segment * S_DEV
        own = lax.dynamic_slice_in_dim(frames, start, S_DEV, 1)
        before = lax.dynamic_slice_in_dim(frames, jnp.maximum(start - (TAPS - 1), 0).astype(jnp.int32), TAPS - 1, 1)
        before = jnp.where(segment > 0, before, jnp.zeros_like(before))
        extended = jnp.concatenate([before, own], axis=1).astype(jnp.float32)
        filtered = weights[0][None, None, :] * extended[:, 0:S_DEV, :]
        for tap in range(1, TAPS):
            filtered = filtered + weights[tap][None, None, :] * extended[:, tap:tap + S_DEV, :]
        spectra = jnp.einsum('isn,nj->ijs', filtered, table, precision=lax.Precision.HIGHEST).astype(jnp.bfloat16)
        spec_f = spectra.astype(jnp.float32).reshape(INPUTS, 2, CHANNELS, S_DEV)
        real_part = jnp.einsum('ipcs,jpcs->icj', spec_f, spec_f)
        imag_part = jnp.einsum('ics,jcs->icj', spec_f[:, 1], spec_f[:, 0]) - jnp.einsum('ics,jcs->icj', spec_f[:, 0], spec_f[:, 1])
        return (total + jnp.stack([real_part, imag_part], axis=1), None)
    start_total = jnp.zeros((INPUTS, 2, CHANNELS, INPUTS), jnp.float32)
    total, _ = lax.scan(block, start_total, jnp.arange(N_TM, dtype=jnp.int32))
    return total * (1.0 / math.sqrt(NSPEC))
```

```python
import functools
import math

import jax
import jax.numpy as jnp
import numpy as np
from jax import lax
from jax.experimental import pallas as pl
from jax.experimental.pallas import tpu as pltpu
from jax.sharding import PartitionSpec as P

MESH = pl.DeviceIdType.MESH
HEAD = 4
STEPS = 32
AHEAD = 10
LAG = 3
RING = 8
LANES = 128


def each(first, end, body):
    def step(d, carry):
        body(d)
        return carry

    lax.fori_loop(first, end, step, 0)


def across(me, mask, n):
    if n & (n - 1):
        return lax.rem(me + mask, n), lax.rem(me + n - mask, n)
    peer, bit = me, 1
    while bit < n:
        flip = lax.rem(mask // bit, 2)
        peer = peer + flip * bit * (1 - 2 * lax.rem(me // bit, 2))
        bit *= 2
    return peer, peer


def correlator(
    n_inp, n_tm, scale, x, weights, table_hbm, out,
    xb, halo, table, low, high, turn, spec, recv, part, got, held,
    x_sem, table_sem, halo_sem, send_sem, recv_sem, own_sem, put_sem, got_sem, out_sem,
):
    me = lax.axis_index("inp")
    seg = lax.axis_index("tm")
    ch_dev, _, _, in_dev, count = recv.shape
    groups, _, _, frame = halo.shape
    rim = halo.shape[1]
    pack = xb.shape[1]
    block = xb.shape[2] - rim
    width = pack * 8
    half = frame // 2
    fold = ch_dev // 2
    inputs = n_inp * in_dev
    rows = inputs // n_tm
    head = max(ch_dev // HEAD, 1)
    per = max(ch_dev // STEPS, 1)
    chunks = 1 + (ch_dev - head) // per
    in_units = in_dev // width
    s_units = count // block
    units = in_units * s_units

    barrier = pltpu.get_barrier_semaphore()
    for d in range(1, n_inp):
        pl.semaphore_signal(
            barrier, inc=1, device_id={"inp": lax.rem(me + d, n_inp)}, device_id_type=MESH
        )
    for d in range(1, n_tm):
        pl.semaphore_signal(
            barrier, inc=1, device_id={"tm": lax.rem(seg + d, n_tm)}, device_id_type=MESH
        )

    def place(u):
        return lax.rem(u, in_units), lax.rem(u // in_units + 1, s_units)

    def inner_load(u):
        g, s = place(u)
        slot = lax.rem(u, 2)
        return pltpu.make_async_copy(
            x.at[pl.ds(g * pack, pack), pl.ds(s * block - rim, block + rim)],
            xb.at[slot], x_sem.at[slot],
        )

    def first_load(u):
        g, _ = place(u)
        slot = lax.rem(u, 2)
        return pltpu.make_async_copy(
            x.at[pl.ds(g * pack, pack), pl.ds(0, block)],
            xb.at[slot, :, pl.ds(rim, block)], x_sem.at[slot],
        )

    def load(u, act):
        _, s = place(u)

        @pl.when(s > 0)
        def _():
            act(inner_load(u))

        @pl.when(s == 0)
        def _():
            act(first_load(u))

    def rim_copy():
        return pltpu.make_async_remote_copy(
            src_ref=x.at[:, pl.ds(count - rim, rim)],
            dst_ref=halo,
            send_sem=halo_sem.at[0],
            recv_sem=halo_sem.at[1],
            device_id={"tm": lax.rem(seg + 1, n_tm)},
            device_id_type=MESH,
        )

    table_copy = pltpu.make_async_copy(table_hbm, table, table_sem.at[0])
    load(0, lambda copy: copy.start())
    table_copy.start()

    def own_head():
        return pltpu.make_async_copy(
            spec.at[me, pl.ds(0, head)], recv.at[pl.ds(0, head), :, me], own_sem.at[0]
        )

    def own_copy(c):
        chunk = pl.ds(head + (c - 1) * per, per)
        return pltpu.make_async_copy(
            spec.at[me, chunk], recv.at[chunk, :, me], own_sem.at[c]
        )

    def remote(mask, c, src, dst):
        return pltpu.make_async_remote_copy(
            src_ref=src,
            dst_ref=dst,
            send_sem=send_sem.at[c, mask - 1],
            recv_sem=recv_sem.at[c, mask - 1],
            device_id={"inp": across(me, mask, n_inp)[0]},
            device_id_type=MESH,
        )

    def unit_copy(u, mask):
        g, s = place(u)
        peer = across(me, mask, n_inp)[0]
        at = pl.ds(pl.multiple_of(g * width, width), width)
        span = pl.ds(pl.multiple_of(s * block, block), block)
        first = pl.ds(0, head)
        return remote(
            mask, 0, spec.at[peer, first, :, at, span], recv.at[first, :, me, at, span]
        )

    def head_copy(mask):
        peer = across(me, mask, n_inp)[0]
        first = pl.ds(0, head)
        return remote(mask, 0, spec.at[peer, first], recv.at[first, :, me])

    def chunk_copy(c, mask):
        peer = across(me, mask, n_inp)[0]
        chunk = pl.ds(head + (c - 1) * per, per)
        return remote(mask, c, spec.at[peer, chunk], recv.at[chunk, :, me])

    def send(c):
        own_copy(c).start()
        each(0, n_inp - 1, lambda k: chunk_copy(c, n_inp - 1 - k).start())

    def filter_unit(u):
        slot = lax.rem(u, 2)
        step = 8

        def some(k):
            g = k // (block // step)
            s = lax.rem(k, block // step) * step
            to = pl.ds(pl.multiple_of((g * block + s) * 8, step * 8), step * 8)
            for t in range(half // LANES):
                sides = []
                for first in (t * LANES, half + t * LANES):
                    lane = slice(first, first + LANES)
                    frames = xb[slot, g, pl.ds(s, step + rim), :, lane].astype(jnp.float32)
                    total = weights[0:1, lane][None] * frames[0:step]
                    for tap in range(1, rim + 1):
                        total = total + weights[tap : tap + 1, lane][None] * frames[tap : tap + step]
                    sides.append(total.reshape(step * 8, LANES))
                low[t, to] = sides[0] + sides[1]
                high[t, to] = sides[0] - sides[1]

        each(0, pack * (block // step), some)

    def transform(folded, odd):
        def pair(k):
            two = []
            for i in (2 * k, 2 * k + 1):
                at = (i // 8) * (block * 8) + lax.rem(i, 8)
                two.append(
                    jnp.concatenate(
                        [folded[t, pl.ds(at, block, stride=8), :] for t in range(half // LANES)],
                        axis=1,
                    )
                )
            value = jnp.concatenate(two, axis=0)
            top = value.astype(jnp.bfloat16)
            rest = (value - top.astype(jnp.float32)).astype(jnp.bfloat16)
            side = lax.dot_general(
                table[odd],
                jnp.concatenate([top, top, rest], axis=1),
                (((1,), (1,)), ((), ())),
                preferred_element_type=jnp.float32,
            )
            for n in range(2):
                turn[pl.ds(2 * k + n, half, stride=width), :] = side[:, n * block : (n + 1) * block]

        each(0, width // 2, pair)

    def spread(u, odd):
        g, s = place(u)
        at = pl.ds(pl.multiple_of(g * width, width), width)
        span = pl.ds(pl.multiple_of(s * block, block), block)
        size = 2 * width

        def some(k):
            rows_in = turn[pl.ds(pl.multiple_of(k * size, size), size), :]
            spec[k // fold, odd * fold + lax.rem(k, fold), :, at, span] = rows_in.astype(
                jnp.bfloat16
            ).reshape(2, width, block)

        each(0, n_inp * fold, some)

    def unit(u):
        @pl.when(u + 1 < units)
        def _():
            load(u + 1, lambda copy: copy.start())

        load(u, lambda copy: copy.wait())
        g, s = place(u)

        @pl.when(s == 0)
        def _():
            @pl.when(jnp.logical_and(seg > 0, u == units - in_units))
            def _():
                rim_copy().wait_recv()

            @pl.when(jnp.logical_and(seg == 0, u == units - in_units))
            def _():
                halo[...] = jnp.zeros_like(halo)

            xb[lax.rem(u, 2), :, 0:rim] = halo[pl.ds(g * pack, pack)]

        filter_unit(u)

        @pl.when(u == 0)
        def _():
            table_copy.wait()

        transform(low, 0)
        spread(u, 0)

        @pl.when(u == 0)
        def _():
            pl.semaphore_wait(barrier, n_inp - 1 + n_tm - 1)

            @pl.when(seg + 1 < n_tm)
            def _():
                rim_copy().start()

        each(0, n_inp - 1, lambda k: unit_copy(u, n_inp - 1 - k).start())
        transform(high, 1)
        spread(u, 1)

    each(0, units, unit)
    own_head().start()

    @pl.when(seg + 1 < n_tm)
    def _():
        rim_copy().wait_send()

    def sum_copy(g, d):
        peer = lax.rem(seg + d, n_tm)
        return pltpu.make_async_remote_copy(
            src_ref=part.at[lax.rem(g, RING), peer],
            dst_ref=got.at[d - 1, g],
            send_sem=put_sem.at[g, d - 1],
            recv_sem=got_sem.at[g, d - 1],
            device_id={"tm": peer},
            device_id_type=MESH,
        )

    def side(ch, p):
        value = recv[ch, p]
        if in_dev % 16 == 0:
            return value.reshape(inputs, count)
        return value.astype(jnp.float32).reshape(inputs, count).astype(jnp.bfloat16)

    def correlate(ch):
        real = side(ch, 0)
        imag = side(ch, 1)
        a = jnp.concatenate([real, imag], axis=1)
        b = jnp.concatenate([imag, -real], axis=1)
        for p, left in ((0, a), (1, b)):
            product = lax.dot_general(
                left, a, (((1,), (1,)), ((), ())), preferred_element_type=jnp.float32
            )
            for q in range(n_tm):
                part[lax.rem(ch, RING), q, p] = product[q * rows : (q + 1) * rows]

    def finish(g):
        each(1, n_tm, lambda d: sum_copy(g, d).wait_recv())
        ch = lax.rem(g, fold) * 2 + g // fold
        for p in range(2):
            total = part[lax.rem(g, RING), seg, p]
            for d in range(1, n_tm):
                total = total + got[d - 1, g, p]
            total = total * scale
            for t in range(inputs // LANES):
                at = pl.ds(p * ch_dev + ch, rows, stride=2 * ch_dev)
                held[t, at, :] = total[:, t * LANES : (t + 1) * LANES]

    def channel(g):
        @pl.when(g >= RING)
        def _():
            each(1, n_tm, lambda d: sum_copy(g - RING, d).wait_send())

        correlate(g)
        each(1, n_tm, lambda d: sum_copy(g, d).start())

        @pl.when(g >= LAG)
        def _():
            finish(g - LAG)

    for c in range(1, min(AHEAD, chunks)):
        send(c)
    own_head().wait()
    each(1, n_inp, lambda mask: head_copy(mask).wait_recv())
    each(0, head, channel)

    def step(c):
        @pl.when(c + AHEAD - 1 < chunks)
        def _():
            send(c + AHEAD - 1)

        own_copy(c).wait()
        each(1, n_inp, lambda mask: chunk_copy(c, mask).wait_recv())
        each(0, per, lambda k: channel(head + (c - 1) * per + k))

    each(1, chunks, step)
    each(max(ch_dev - LAG, 0), ch_dev, finish)
    out_copies = [
        pltpu.make_async_copy(held.at[t], out.at[:, pl.ds(t * LANES, LANES)], out_sem.at[t])
        for t in range(inputs // LANES)
    ]
    for copy in out_copies:
        copy.start()
    each(1, n_inp, lambda mask: head_copy(mask).wait_send())
    each(1, chunks, lambda c: each(1, n_inp, lambda mask: chunk_copy(c, mask).wait_send()))
    each(
        max(ch_dev - RING, 0),
        ch_dev,
        lambda g: each(1, n_tm, lambda d: sum_copy(g, d).wait_send()),
    )
    for copy in out_copies:
        copy.wait()


def tables(frame):
    fold = frame // 2
    sides = []
    for odd in (0, 1):
        column = np.arange(fold)
        channel = column // 2 * 2 + odd
        phase = np.arange(fold)[:, None] * channel[None, :] % frame
        angle = phase * (2.0 * math.pi / frame)
        whole = np.where(column % 2 == 0, np.cos(angle), -np.sin(angle)) * frame ** (-0.5)
        whole = whole.T.astype(np.float32)
        top = whole.astype(jnp.bfloat16)
        rest = (whole - top.astype(np.float32)).astype(jnp.bfloat16)
        sides.append(np.concatenate([top, rest, top], axis=1))
    return np.stack(sides)


def per_device(samples, tap_weights):
    in_dev = samples.shape[0]
    taps, frame = tap_weights.shape
    rim = taps - 1
    count = samples.shape[1] // frame
    n_inp = lax.axis_size("inp")
    n_tm = lax.axis_size("tm")
    ch_dev = frame // 2 // n_inp
    inputs = n_inp * in_dev
    rows = inputs // n_tm
    groups = in_dev // 8
    pack = math.gcd(groups, 2)
    block = LANES
    head = max(ch_dev // HEAD, 1)
    per = max(ch_dev // STEPS, 1)
    chunks = 1 + (ch_dev - head) // per
    scale = 1.0 / math.sqrt(count * n_tm)
    frames = samples.reshape(groups, 8, count, frame).transpose(0, 2, 1, 3)
    mine = pl.pallas_call(
        functools.partial(correlator, n_inp, n_tm, scale),
        out_shape=jax.ShapeDtypeStruct((rows * 2 * ch_dev, inputs), jnp.float32),
        in_specs=[
            pl.BlockSpec(memory_space=pltpu.HBM),
            pl.BlockSpec(memory_space=pltpu.VMEM),
            pl.BlockSpec(memory_space=pltpu.HBM),
        ],
        out_specs=pl.BlockSpec(memory_space=pltpu.HBM),
        scratch_shapes=[
            pltpu.VMEM((2, pack, block + rim, 8, frame), jnp.bfloat16),
            pltpu.VMEM((groups, rim, 8, frame), jnp.bfloat16),
            pltpu.VMEM((2, frame // 2, 3 * (frame // 2)), jnp.bfloat16),
            pltpu.VMEM((frame // 2 // LANES, pack * block * 8, LANES), jnp.float32),
            pltpu.VMEM((frame // 2 // LANES, pack * block * 8, LANES), jnp.float32),
            pltpu.VMEM((frame // 2 * pack * 8, block), jnp.float32),
            pltpu.VMEM((n_inp, ch_dev, 2, in_dev, count), jnp.bfloat16),
            pltpu.VMEM((ch_dev, 2, n_inp, in_dev, count), jnp.bfloat16),
            pltpu.VMEM((RING, n_tm, 2, rows, inputs), jnp.float32),
            pltpu.VMEM((n_tm - 1, ch_dev, 2, rows, inputs), jnp.float32),
            pltpu.VMEM((inputs // LANES, rows * 2 * ch_dev, LANES), jnp.float32),
            pltpu.SemaphoreType.DMA((2,)),
            pltpu.SemaphoreType.DMA((1,)),
            pltpu.SemaphoreType.DMA((2,)),
            pltpu.SemaphoreType.DMA((chunks, n_inp - 1)),
            pltpu.SemaphoreType.DMA((chunks, n_inp - 1)),
            pltpu.SemaphoreType.DMA((chunks,)),
            pltpu.SemaphoreType.DMA((ch_dev, n_tm - 1)),
            pltpu.SemaphoreType.DMA((ch_dev, n_tm - 1)),
            pltpu.SemaphoreType.DMA((inputs // LANES,)),
        ],
        compiler_params=pltpu.CompilerParams(
            collective_id=0, has_side_effects=True, vmem_limit_bytes=63 << 20
        ),
    )(frames, tap_weights, jnp.asarray(tables(frame)))
    return mine.reshape(rows, 2, ch_dev, inputs)


def solution(mesh):
    return jax.shard_map(
        per_device,
        mesh=mesh,
        in_specs=(P("inp", "tm"), P()),
        out_specs=P("tm", None, "inp", None),
        check_vma=False,
    )
```

```python
import functools
import math

import jax
import jax.numpy as jnp
import numpy as np
from jax import lax
from jax.experimental import pallas as pl
from jax.experimental.pallas import tpu as pltpu
from jax.sharding import PartitionSpec as P

MESH = pl.DeviceIdType.MESH
HEAD = 4
STEPS = 32
OUTER = 2
INNER = 8
LATE = 8
SOON = 2
RING = 12
LANES = 128


def each(first, end, body):
    def step(d, carry):
        body(d)
        return carry

    lax.fori_loop(first, end, step, 0)


def across(me, mask, n):
    if n & (n - 1):
        return lax.rem(me + mask, n), lax.rem(me + n - mask, n)
    peer, bit = me, 1
    while bit < n:
        flip = lax.rem(mask // bit, 2)
        peer = peer + flip * bit * (1 - 2 * lax.rem(me // bit, 2))
        bit *= 2
    return peer, peer


def correlator(
    n_inp, n_tm, scale, x, weights, table_hbm, out,
    xb, halo, table, low, high, turn, spec, recv, part, got, held,
    x_sem, table_sem, halo_sem, send_sem, recv_sem, own_sem, put_sem, got_sem, out_sem,
):
    me = lax.axis_index("inp")
    seg = lax.axis_index("tm")
    ch_dev, _, _, in_dev, count = recv.shape
    groups, _, _, frame = halo.shape
    rim = halo.shape[1]
    pack = xb.shape[1]
    block = xb.shape[2] - rim
    width = pack * 8
    half = frame // 2
    fold = ch_dev // 2
    inputs = n_inp * in_dev
    rows = inputs // n_tm
    head = max(ch_dev // HEAD, 1)
    per = max(ch_dev // STEPS, 1)
    chunks = 1 + (ch_dev - head) // per
    in_units = in_dev // width
    s_units = count // block
    units = in_units * s_units

    barrier = pltpu.get_barrier_semaphore()
    for d in range(1, n_inp):
        pl.semaphore_signal(
            barrier, inc=1, device_id={"inp": lax.rem(me + d, n_inp)}, device_id_type=MESH
        )
    for d in range(1, n_tm):
        pl.semaphore_signal(
            barrier, inc=1, device_id={"tm": lax.rem(seg + d, n_tm)}, device_id_type=MESH
        )

    def place(u):
        return lax.rem(u, in_units), lax.rem(u // in_units + 1, s_units)

    def inner_load(u):
        g, s = place(u)
        slot = lax.rem(u, 2)
        return pltpu.make_async_copy(
            x.at[pl.ds(g * pack, pack), pl.ds(s * block - rim, block + rim)],
            xb.at[slot], x_sem.at[slot],
        )

    def first_load(u):
        g, _ = place(u)
        slot = lax.rem(u, 2)
        return pltpu.make_async_copy(
            x.at[pl.ds(g * pack, pack), pl.ds(0, block)],
            xb.at[slot, :, pl.ds(rim, block)], x_sem.at[slot],
        )

    def load(u, act):
        _, s = place(u)

        @pl.when(s > 0)
        def _():
            act(inner_load(u))

        @pl.when(s == 0)
        def _():
            act(first_load(u))

    def rim_copy():
        return pltpu.make_async_remote_copy(
            src_ref=x.at[:, pl.ds(count - rim, rim)],
            dst_ref=halo,
            send_sem=halo_sem.at[0],
            recv_sem=halo_sem.at[1],
            device_id={"tm": lax.rem(seg + 1, n_tm)},
            device_id_type=MESH,
        )

    table_copy = pltpu.make_async_copy(table_hbm, table, table_sem.at[0])
    load(0, lambda copy: copy.start())
    table_copy.start()

    def own_head():
        return pltpu.make_async_copy(
            spec.at[me, pl.ds(0, head)], recv.at[pl.ds(0, head), :, me], own_sem.at[0]
        )

    def own_copy(c):
        chunk = pl.ds(head + (c - 1) * per, per)
        return pltpu.make_async_copy(
            spec.at[me, chunk], recv.at[chunk, :, me], own_sem.at[c]
        )

    def remote(mask, c, src, dst):
        return pltpu.make_async_remote_copy(
            src_ref=src,
            dst_ref=dst,
            send_sem=send_sem.at[c, mask - 1],
            recv_sem=recv_sem.at[c, mask - 1],
            device_id={"inp": across(me, mask, n_inp)[0]},
            device_id_type=MESH,
        )

    def unit_copy(u, mask):
        g, s = place(u)
        peer = across(me, mask, n_inp)[0]
        at = pl.ds(pl.multiple_of(g * width, width), width)
        span = pl.ds(pl.multiple_of(s * block, block), block)
        first = pl.ds(0, head)
        return remote(
            mask, 0, spec.at[peer, first, :, at, span], recv.at[first, :, me, at, span]
        )

    def head_copy(mask):
        peer = across(me, mask, n_inp)[0]
        first = pl.ds(0, head)
        return remote(mask, 0, spec.at[peer, first], recv.at[first, :, me])

    def chunk_copy(c, mask):
        peer = across(me, mask, n_inp)[0]
        chunk = pl.ds(head + (c - 1) * per, per)
        return remote(mask, c, spec.at[peer, chunk], recv.at[chunk, :, me])

    def send(c):
        own_copy(c).start()
        each(0, n_inp - 1, lambda k: chunk_copy(c, n_inp - 1 - k).start())

    def filter_unit(u):
        slot = lax.rem(u, 2)
        step = 8

        def some(k):
            g = k // (block // step)
            s = lax.rem(k, block // step) * step
            to = pl.ds(pl.multiple_of((g * block + s) * 8, step * 8), step * 8)
            for t in range(half // LANES):
                sides = []
                for first in (t * LANES, half + t * LANES):
                    lane = slice(first, first + LANES)
                    frames = xb[slot, g, pl.ds(s, step + rim), :, lane].astype(jnp.float32)
                    total = weights[0:1, lane][None] * frames[0:step]
                    for tap in range(1, rim + 1):
                        total = total + weights[tap : tap + 1, lane][None] * frames[tap : tap + step]
                    sides.append(total.reshape(step * 8, LANES))
                low[t, to] = sides[0] + sides[1]
                high[t, to] = sides[0] - sides[1]

        each(0, pack * (block // step), some)

    def transform(folded, odd):
        def pair(k):
            two = []
            for i in (2 * k, 2 * k + 1):
                at = (i // 8) * (block * 8) + lax.rem(i, 8)
                two.append(
                    jnp.concatenate(
                        [folded[t, pl.ds(at, block, stride=8), :] for t in range(half // LANES)],
                        axis=1,
                    )
                )
            value = jnp.concatenate(two, axis=0)
            top = value.astype(jnp.bfloat16)
            rest = (value - top.astype(jnp.float32)).astype(jnp.bfloat16)
            side = lax.dot_general(
                table[odd],
                jnp.concatenate([top, top, rest], axis=1),
                (((1,), (1,)), ((), ())),
                preferred_element_type=jnp.float32,
            )
            for n in range(2):
                turn[pl.ds(2 * k + n, half, stride=width), :] = side[:, n * block : (n + 1) * block]

        each(0, width // 2, pair)

    def spread(u, odd):
        g, s = place(u)
        at = pl.ds(pl.multiple_of(g * width, width), width)
        span = pl.ds(pl.multiple_of(s * block, block), block)
        size = 2 * width

        def some(k):
            rows_in = turn[pl.ds(pl.multiple_of(k * size, size), size), :]
            spec[k // fold, odd * fold + lax.rem(k, fold), :, at, span] = rows_in.astype(
                jnp.bfloat16
            ).reshape(2, width, block)

        each(0, n_inp * fold, some)

    def unit(u):
        @pl.when(u + 1 < units)
        def _():
            load(u + 1, lambda copy: copy.start())

        load(u, lambda copy: copy.wait())
        g, s = place(u)

        @pl.when(s == 0)
        def _():
            @pl.when(jnp.logical_and(seg > 0, u == units - in_units))
            def _():
                rim_copy().wait_recv()

            @pl.when(jnp.logical_and(seg == 0, u == units - in_units))
            def _():
                halo[...] = jnp.zeros_like(halo)

            xb[lax.rem(u, 2), :, 0:rim] = halo[pl.ds(g * pack, pack)]

        filter_unit(u)

        @pl.when(u == 0)
        def _():
            table_copy.wait()

        transform(low, 0)
        spread(u, 0)

        @pl.when(u == 0)
        def _():
            pl.semaphore_wait(barrier, n_inp - 1 + n_tm - 1)

            @pl.when(seg + 1 < n_tm)
            def _():
                rim_copy().start()

        each(0, n_inp - 1, lambda k: unit_copy(u, n_inp - 1 - k).start())
        transform(high, 1)
        spread(u, 1)

    each(0, units, unit)
    own_head().start()

    @pl.when(seg + 1 < n_tm)
    def _():
        rim_copy().wait_send()

    def sum_copy(g, d):
        peer = lax.rem(seg + d, n_tm)
        return pltpu.make_async_remote_copy(
            src_ref=part.at[lax.rem(g, RING), peer],
            dst_ref=got.at[d - 1, g],
            send_sem=put_sem.at[g, d - 1],
            recv_sem=got_sem.at[g, d - 1],
            device_id={"tm": peer},
            device_id_type=MESH,
        )

    def side(ch, p):
        value = recv[ch, p]
        if in_dev % 16 == 0:
            return value.reshape(inputs, count)
        return value.astype(jnp.float32).reshape(inputs, count).astype(jnp.bfloat16)

    def correlate(ch):
        real = side(ch, 0)
        imag = side(ch, 1)
        a = jnp.concatenate([real, imag], axis=1)
        b = jnp.concatenate([imag, -real], axis=1)
        for p, left in ((0, a), (1, b)):
            product = lax.dot_general(
                left, a, (((1,), (1,)), ((), ())), preferred_element_type=jnp.float32
            )
            for q in range(n_tm):
                part[lax.rem(ch, RING), q, p] = product[q * rows : (q + 1) * rows]

    def finish(g):
        each(1, n_tm, lambda d: sum_copy(g, d).wait_recv())
        ch = lax.rem(g, fold) * 2 + g // fold
        for p in range(2):
            total = part[lax.rem(g, RING), seg, p]
            for d in range(1, n_tm):
                total = total + got[d - 1, g, p]
            total = total * scale
            for t in range(inputs // LANES):
                at = pl.ds(p * ch_dev + ch, rows, stride=2 * ch_dev)
                held[t, at, :] = total[:, t * LANES : (t + 1) * LANES]

    def done(g):
        early = g + 1 - LATE
        late = ch_dev - SOON - 2 * (ch_dev - 1 - g)
        return jnp.maximum(jnp.maximum(early, late), 0)

    def channel(g):
        @pl.when(g >= RING)
        def _():
            each(1, n_tm, lambda d: sum_copy(g - RING, d).wait_send())

        correlate(g)
        each(1, n_tm, lambda d: sum_copy(g, d).start())

        each(done(g - 1), done(g), finish)

    ring = me // max(n_inp // 4, 1)
    ahead = jnp.where(jnp.logical_and(ring > 0, ring < 3), INNER, OUTER)
    each(1, jnp.minimum(ahead, chunks), send)
    own_head().wait()
    each(1, n_inp, lambda mask: head_copy(mask).wait_recv())
    each(0, head, channel)

    def step(c):
        @pl.when(c + ahead - 1 < chunks)
        def _():
            send(c + ahead - 1)

        own_copy(c).wait()
        each(1, n_inp, lambda mask: chunk_copy(c, mask).wait_recv())
        each(0, per, lambda k: channel(head + (c - 1) * per + k))

    each(1, chunks, step)
    each(done(ch_dev - 1), ch_dev, finish)
    out_copies = [
        pltpu.make_async_copy(held.at[t], out.at[:, pl.ds(t * LANES, LANES)], out_sem.at[t])
        for t in range(inputs // LANES)
    ]
    for copy in out_copies:
        copy.start()
    each(1, n_inp, lambda mask: head_copy(mask).wait_send())
    each(1, chunks, lambda c: each(1, n_inp, lambda mask: chunk_copy(c, mask).wait_send()))
    each(
        max(ch_dev - RING, 0),
        ch_dev,
        lambda g: each(1, n_tm, lambda d: sum_copy(g, d).wait_send()),
    )
    for copy in out_copies:
        copy.wait()


def tables(frame):
    fold = frame // 2
    sides = []
    for odd in (0, 1):
        column = np.arange(fold)
        channel = column // 2 * 2 + odd
        phase = np.arange(fold)[:, None] * channel[None, :] % frame
        angle = phase * (2.0 * math.pi / frame)
        whole = np.where(column % 2 == 0, np.cos(angle), -np.sin(angle)) * frame ** (-0.5)
        whole = whole.T.astype(np.float32)
        top = whole.astype(jnp.bfloat16)
        rest = (whole - top.astype(np.float32)).astype(jnp.bfloat16)
        sides.append(np.concatenate([top, rest, top], axis=1))
    return np.stack(sides)


def per_device(samples, tap_weights):
    in_dev = samples.shape[0]
    taps, frame = tap_weights.shape
    rim = taps - 1
    count = samples.shape[1] // frame
    n_inp = lax.axis_size("inp")
    n_tm = lax.axis_size("tm")
    ch_dev = frame // 2 // n_inp
    inputs = n_inp * in_dev
    rows = inputs // n_tm
    groups = in_dev // 8
    pack = math.gcd(groups, 2)
    block = LANES
    head = max(ch_dev // HEAD, 1)
    per = max(ch_dev // STEPS, 1)
    chunks = 1 + (ch_dev - head) // per
    scale = 1.0 / math.sqrt(count * n_tm)
    frames = samples.reshape(groups, 8, count, frame).transpose(0, 2, 1, 3)
    mine = pl.pallas_call(
        functools.partial(correlator, n_inp, n_tm, scale),
        out_shape=jax.ShapeDtypeStruct((rows * 2 * ch_dev, inputs), jnp.float32),
        in_specs=[
            pl.BlockSpec(memory_space=pltpu.HBM),
            pl.BlockSpec(memory_space=pltpu.VMEM),
            pl.BlockSpec(memory_space=pltpu.HBM),
        ],
        out_specs=pl.BlockSpec(memory_space=pltpu.HBM),
        scratch_shapes=[
            pltpu.VMEM((2, pack, block + rim, 8, frame), jnp.bfloat16),
            pltpu.VMEM((groups, rim, 8, frame), jnp.bfloat16),
            pltpu.VMEM((2, frame // 2, 3 * (frame // 2)), jnp.bfloat16),
            pltpu.VMEM((frame // 2 // LANES, pack * block * 8, LANES), jnp.float32),
            pltpu.VMEM((frame // 2 // LANES, pack * block * 8, LANES), jnp.float32),
            pltpu.VMEM((frame // 2 * pack * 8, block), jnp.float32),
            pltpu.VMEM((n_inp, ch_dev, 2, in_dev, count), jnp.bfloat16),
            pltpu.VMEM((ch_dev, 2, n_inp, in_dev, count), jnp.bfloat16),
            pltpu.VMEM((RING, n_tm, 2, rows, inputs), jnp.float32),
            pltpu.VMEM((n_tm - 1, ch_dev, 2, rows, inputs), jnp.float32),
            pltpu.VMEM((inputs // LANES, rows * 2 * ch_dev, LANES), jnp.float32),
            pltpu.SemaphoreType.DMA((2,)),
            pltpu.SemaphoreType.DMA((1,)),
            pltpu.SemaphoreType.DMA((2,)),
            pltpu.SemaphoreType.DMA((chunks, n_inp - 1)),
            pltpu.SemaphoreType.DMA((chunks, n_inp - 1)),
            pltpu.SemaphoreType.DMA((chunks,)),
            pltpu.SemaphoreType.DMA((ch_dev, n_tm - 1)),
            pltpu.SemaphoreType.DMA((ch_dev, n_tm - 1)),
            pltpu.SemaphoreType.DMA((inputs // LANES,)),
        ],
        compiler_params=pltpu.CompilerParams(
            collective_id=0, has_side_effects=True, vmem_limit_bytes=63 << 20
        ),
    )(frames, tap_weights, jnp.asarray(tables(frame)))
    return mine.reshape(rows, 2, ch_dev, inputs)


def solution(mesh):
    return jax.shard_map(
        per_device,
        mesh=mesh,
        in_specs=(P("inp", "tm"), P()),
        out_specs=P("tm", None, "inp", None),
        check_vma=False,
    )
```

```python
import functools
import math

import jax
import jax.numpy as jnp
import numpy as np
from jax import lax
from jax.experimental import pallas as pl
from jax.experimental.pallas import tpu as pltpu
from jax.sharding import PartitionSpec as P

MESH = pl.DeviceIdType.MESH
HEAD = 4
STEPS = 32
OUTER = 1
INNER = 8
LATE = 8
SOON = 2
RING = 12
LANES = 128


def each(first, end, body):
    def step(d, carry):
        body(d)
        return carry

    lax.fori_loop(first, end, step, 0)


def across(me, mask, n):
    if n & (n - 1):
        return lax.rem(me + mask, n), lax.rem(me + n - mask, n)
    peer, bit = me, 1
    while bit < n:
        flip = lax.rem(mask // bit, 2)
        peer = peer + flip * bit * (1 - 2 * lax.rem(me // bit, 2))
        bit *= 2
    return peer, peer


def correlator(
    n_inp, n_tm, scale, x, weights, table_hbm, out,
    xb, halo, table, low, high, turn, spec, recv, part, got, held,
    x_sem, table_sem, halo_sem, send_sem, recv_sem, own_sem, put_sem, got_sem, out_sem,
):
    me = lax.axis_index("inp")
    seg = lax.axis_index("tm")
    ch_dev, _, _, in_dev, count = recv.shape
    groups, _, _, frame = halo.shape
    rim = halo.shape[1]
    pack = xb.shape[1]
    block = xb.shape[2] - rim
    width = pack * 8
    half = frame // 2
    fold = ch_dev // 2
    inputs = n_inp * in_dev
    rows = inputs // n_tm
    head = max(ch_dev // HEAD, 1)
    per = max(ch_dev // STEPS, 1)
    chunks = 1 + (ch_dev - head) // per
    in_units = in_dev // width
    s_units = count // block
    units = in_units * s_units

    barrier = pltpu.get_barrier_semaphore()
    for d in range(1, n_inp):
        pl.semaphore_signal(
            barrier, inc=1, device_id={"inp": lax.rem(me + d, n_inp)}, device_id_type=MESH
        )
    for d in range(1, n_tm):
        pl.semaphore_signal(
            barrier, inc=1, device_id={"tm": lax.rem(seg + d, n_tm)}, device_id_type=MESH
        )

    def place(u):
        return lax.rem(u, in_units), lax.rem(u // in_units + 1, s_units)

    def inner_load(u):
        g, s = place(u)
        slot = lax.rem(u, 2)
        return pltpu.make_async_copy(
            x.at[pl.ds(g * pack, pack), pl.ds(s * block - rim, block + rim)],
            xb.at[slot], x_sem.at[slot],
        )

    def first_load(u):
        g, _ = place(u)
        slot = lax.rem(u, 2)
        return pltpu.make_async_copy(
            x.at[pl.ds(g * pack, pack), pl.ds(0, block)],
            xb.at[slot, :, pl.ds(rim, block)], x_sem.at[slot],
        )

    def load(u, act):
        _, s = place(u)

        @pl.when(s > 0)
        def _():
            act(inner_load(u))

        @pl.when(s == 0)
        def _():
            act(first_load(u))

    def rim_copy():
        return pltpu.make_async_remote_copy(
            src_ref=x.at[:, pl.ds(count - rim, rim)],
            dst_ref=halo,
            send_sem=halo_sem.at[0],
            recv_sem=halo_sem.at[1],
            device_id={"tm": lax.rem(seg + 1, n_tm)},
            device_id_type=MESH,
        )

    table_copy = pltpu.make_async_copy(table_hbm, table, table_sem.at[0])
    load(0, lambda copy: copy.start())
    table_copy.start()

    def own_head():
        return pltpu.make_async_copy(
            spec.at[me, pl.ds(0, head)], recv.at[pl.ds(0, head), :, me], own_sem.at[0]
        )

    def own_copy(c):
        chunk = pl.ds(head + (c - 1) * per, per)
        return pltpu.make_async_copy(
            spec.at[me, chunk], recv.at[chunk, :, me], own_sem.at[c]
        )

    def remote(mask, c, src, dst):
        return pltpu.make_async_remote_copy(
            src_ref=src,
            dst_ref=dst,
            send_sem=send_sem.at[c, mask - 1],
            recv_sem=recv_sem.at[c, mask - 1],
            device_id={"inp": across(me, mask, n_inp)[0]},
            device_id_type=MESH,
        )

    def unit_copy(u, mask):
        g, s = place(u)
        peer = across(me, mask, n_inp)[0]
        at = pl.ds(pl.multiple_of(g * width, width), width)
        span = pl.ds(pl.multiple_of(s * block, block), block)
        first = pl.ds(0, head)
        return remote(
            mask, 0, spec.at[peer, first, :, at, span], recv.at[first, :, me, at, span]
        )

    def head_copy(mask):
        peer = across(me, mask, n_inp)[0]
        first = pl.ds(0, head)
        return remote(mask, 0, spec.at[peer, first], recv.at[first, :, me])

    def chunk_copy(c, mask):
        peer = across(me, mask, n_inp)[0]
        chunk = pl.ds(head + (c - 1) * per, per)
        return remote(mask, c, spec.at[peer, chunk], recv.at[chunk, :, me])

    def send(c):
        own_copy(c).start()
        each(0, n_inp - 1, lambda k: chunk_copy(c, n_inp - 1 - k).start())

    def filter_unit(u):
        slot = lax.rem(u, 2)
        step = 8

        def some(k):
            g = k // (block // step)
            s = lax.rem(k, block // step) * step
            to = pl.ds(pl.multiple_of((g * block + s) * 8, step * 8), step * 8)
            for t in range(half // LANES):
                sides = []
                for first in (t * LANES, half + t * LANES):
                    lane = slice(first, first + LANES)
                    frames = xb[slot, g, pl.ds(s, step + rim), :, lane].astype(jnp.float32)
                    total = weights[0:1, lane][None] * frames[0:step]
                    for tap in range(1, rim + 1):
                        total = total + weights[tap : tap + 1, lane][None] * frames[tap : tap + step]
                    sides.append(total.reshape(step * 8, LANES))
                low[t, to] = sides[0] + sides[1]
                high[t, to] = sides[0] - sides[1]

        each(0, pack * (block // step), some)

    def transform(folded, odd):
        def pair(k):
            two = []
            for i in (2 * k, 2 * k + 1):
                at = (i // 8) * (block * 8) + lax.rem(i, 8)
                two.append(
                    jnp.concatenate(
                        [folded[t, pl.ds(at, block, stride=8), :] for t in range(half // LANES)],
                        axis=1,
                    )
                )
            value = jnp.concatenate(two, axis=0)
            top = value.astype(jnp.bfloat16)
            rest = (value - top.astype(jnp.float32)).astype(jnp.bfloat16)
            side = lax.dot_general(
                table[odd],
                jnp.concatenate([top, top, rest], axis=1),
                (((1,), (1,)), ((), ())),
                preferred_element_type=jnp.float32,
            )
            for n in range(2):
                turn[pl.ds(2 * k + n, half, stride=width), :] = side[:, n * block : (n + 1) * block]

        def several(k):
            for n in range(together):
                pair(together * k + n)

        pairs = width // 2
        together = math.gcd(pairs, 4)
        each(0, pairs // together, several)

    def spread(u, odd):
        g, s = place(u)
        at = pl.ds(pl.multiple_of(g * width, width), width)
        span = pl.ds(pl.multiple_of(s * block, block), block)
        lot = math.gcd(fold, 8)
        lots = fold // lot
        size = lot * 2 * width

        def some(k):
            rows_in = turn[pl.ds(pl.multiple_of(k * size, size), size), :]
            to = pl.ds(odd * fold + lax.rem(k, lots) * lot, lot)
            spec[k // lots, to, :, at, span] = rows_in.astype(jnp.bfloat16).reshape(
                lot, 2, width, block
            )

        each(0, n_inp * lots, some)

    def unit(u):
        @pl.when(u + 1 < units)
        def _():
            load(u + 1, lambda copy: copy.start())

        load(u, lambda copy: copy.wait())
        g, s = place(u)

        @pl.when(s == 0)
        def _():
            @pl.when(jnp.logical_and(seg > 0, u == units - in_units))
            def _():
                rim_copy().wait_recv()

            @pl.when(jnp.logical_and(seg == 0, u == units - in_units))
            def _():
                halo[...] = jnp.zeros_like(halo)

            xb[lax.rem(u, 2), :, 0:rim] = halo[pl.ds(g * pack, pack)]

        filter_unit(u)

        @pl.when(u == 0)
        def _():
            table_copy.wait()

        transform(low, 0)
        spread(u, 0)

        @pl.when(u == 0)
        def _():
            pl.semaphore_wait(barrier, n_inp - 1 + n_tm - 1)

            @pl.when(seg + 1 < n_tm)
            def _():
                rim_copy().start()

        each(0, n_inp - 1, lambda k: unit_copy(u, n_inp - 1 - k).start())
        transform(high, 1)
        spread(u, 1)

    each(0, units, unit)
    own_head().start()

    @pl.when(seg + 1 < n_tm)
    def _():
        rim_copy().wait_send()

    def sum_copy(g, d):
        peer = lax.rem(seg + d, n_tm)
        return pltpu.make_async_remote_copy(
            src_ref=part.at[lax.rem(g, RING), peer],
            dst_ref=got.at[d - 1, g],
            send_sem=put_sem.at[g, d - 1],
            recv_sem=got_sem.at[g, d - 1],
            device_id={"tm": peer},
            device_id_type=MESH,
        )

    def side(ch, p):
        value = recv[ch, p]
        if in_dev % 16 == 0:
            return value.reshape(inputs, count)
        return value.astype(jnp.float32).reshape(inputs, count).astype(jnp.bfloat16)

    def correlate(ch):
        real = side(ch, 0)
        imag = side(ch, 1)
        a = jnp.concatenate([real, imag], axis=1)
        b = jnp.concatenate([imag, -real], axis=1)
        for p, left in ((0, a), (1, b)):
            product = lax.dot_general(
                left, a, (((1,), (1,)), ((), ())), preferred_element_type=jnp.float32
            )
            for q in range(n_tm):
                part[lax.rem(ch, RING), q, p] = product[q * rows : (q + 1) * rows]

    def finish(g):
        each(1, n_tm, lambda d: sum_copy(g, d).wait_recv())
        ch = lax.rem(g, fold) * 2 + g // fold
        for p in range(2):
            total = part[lax.rem(g, RING), seg, p]
            for d in range(1, n_tm):
                total = total + got[d - 1, g, p]
            total = total * scale
            for t in range(inputs // LANES):
                at = pl.ds(p * ch_dev + ch, rows, stride=2 * ch_dev)
                held[t, at, :] = total[:, t * LANES : (t + 1) * LANES]

    def done(g):
        early = g + 1 - LATE
        late = ch_dev - SOON - 2 * (ch_dev - 1 - g)
        return jnp.maximum(jnp.maximum(early, late), 0)

    def channel(g):
        @pl.when(g >= RING)
        def _():
            each(1, n_tm, lambda d: sum_copy(g - RING, d).wait_send())

        correlate(g)
        each(1, n_tm, lambda d: sum_copy(g, d).start())

        each(done(g - 1), done(g), finish)

    ring = me // max(n_inp // 4, 1)
    ahead = jnp.where(jnp.logical_and(ring > 0, ring < 3), INNER, OUTER)
    each(1, jnp.minimum(ahead, chunks), send)
    own_head().wait()
    each(1, n_inp, lambda mask: head_copy(mask).wait_recv())
    each(0, head, channel)

    def step(c):
        @pl.when(c + ahead - 1 < chunks)
        def _():
            send(c + ahead - 1)

        own_copy(c).wait()
        each(1, n_inp, lambda mask: chunk_copy(c, mask).wait_recv())
        each(0, per, lambda k: channel(head + (c - 1) * per + k))

    each(1, chunks, step)
    each(done(ch_dev - 1), ch_dev, finish)
    out_copies = [
        pltpu.make_async_copy(held.at[t], out.at[:, pl.ds(t * LANES, LANES)], out_sem.at[t])
        for t in range(inputs // LANES)
    ]
    for copy in out_copies:
        copy.start()
    each(1, n_inp, lambda mask: head_copy(mask).wait_send())
    each(1, chunks, lambda c: each(1, n_inp, lambda mask: chunk_copy(c, mask).wait_send()))
    each(
        max(ch_dev - RING, 0),
        ch_dev,
        lambda g: each(1, n_tm, lambda d: sum_copy(g, d).wait_send()),
    )
    for copy in out_copies:
        copy.wait()


def tables(frame):
    fold = frame // 2
    sides = []
    for odd in (0, 1):
        column = np.arange(fold)
        channel = column // 2 * 2 + odd
        phase = np.arange(fold)[:, None] * channel[None, :] % frame
        angle = phase * (2.0 * math.pi / frame)
        whole = np.where(column % 2 == 0, np.cos(angle), -np.sin(angle)) * frame ** (-0.5)
        whole = whole.T.astype(np.float32)
        top = whole.astype(jnp.bfloat16)
        rest = (whole - top.astype(np.float32)).astype(jnp.bfloat16)
        sides.append(np.concatenate([top, rest, top], axis=1))
    return np.stack(sides)


def per_device(samples, tap_weights):
    in_dev = samples.shape[0]
    taps, frame = tap_weights.shape
    rim = taps - 1
    count = samples.shape[1] // frame
    n_inp = lax.axis_size("inp")
    n_tm = lax.axis_size("tm")
    ch_dev = frame // 2 // n_inp
    inputs = n_inp * in_dev
    rows = inputs // n_tm
    groups = in_dev // 8
    pack = math.gcd(groups, 2)
    block = LANES
    head = max(ch_dev // HEAD, 1)
    per = max(ch_dev // STEPS, 1)
    chunks = 1 + (ch_dev - head) // per
    scale = 1.0 / math.sqrt(count * n_tm)
    frames = samples.reshape(groups, 8, count, frame).transpose(0, 2, 1, 3)
    mine = pl.pallas_call(
        functools.partial(correlator, n_inp, n_tm, scale),
        out_shape=jax.ShapeDtypeStruct((rows * 2 * ch_dev, inputs), jnp.float32),
        in_specs=[
            pl.BlockSpec(memory_space=pltpu.HBM),
            pl.BlockSpec(memory_space=pltpu.VMEM),
            pl.BlockSpec(memory_space=pltpu.HBM),
        ],
        out_specs=pl.BlockSpec(memory_space=pltpu.HBM),
        scratch_shapes=[
            pltpu.VMEM((2, pack, block + rim, 8, frame), jnp.bfloat16),
            pltpu.VMEM((groups, rim, 8, frame), jnp.bfloat16),
            pltpu.VMEM((2, frame // 2, 3 * (frame // 2)), jnp.bfloat16),
            pltpu.VMEM((frame // 2 // LANES, pack * block * 8, LANES), jnp.float32),
            pltpu.VMEM((frame // 2 // LANES, pack * block * 8, LANES), jnp.float32),
            pltpu.VMEM((frame // 2 * pack * 8, block), jnp.float32),
            pltpu.VMEM((n_inp, ch_dev, 2, in_dev, count), jnp.bfloat16),
            pltpu.VMEM((ch_dev, 2, n_inp, in_dev, count), jnp.bfloat16),
            pltpu.VMEM((RING, n_tm, 2, rows, inputs), jnp.float32),
            pltpu.VMEM((n_tm - 1, ch_dev, 2, rows, inputs), jnp.float32),
            pltpu.VMEM((inputs // LANES, rows * 2 * ch_dev, LANES), jnp.float32),
            pltpu.SemaphoreType.DMA((2,)),
            pltpu.SemaphoreType.DMA((1,)),
            pltpu.SemaphoreType.DMA((2,)),
            pltpu.SemaphoreType.DMA((chunks, n_inp - 1)),
            pltpu.SemaphoreType.DMA((chunks, n_inp - 1)),
            pltpu.SemaphoreType.DMA((chunks,)),
            pltpu.SemaphoreType.DMA((ch_dev, n_tm - 1)),
            pltpu.SemaphoreType.DMA((ch_dev, n_tm - 1)),
            pltpu.SemaphoreType.DMA((inputs // LANES,)),
        ],
        compiler_params=pltpu.CompilerParams(
            collective_id=0, has_side_effects=True, vmem_limit_bytes=63 << 20
        ),
    )(frames, tap_weights, jnp.asarray(tables(frame)))
    return mine.reshape(rows, 2, ch_dev, inputs)


def solution(mesh):
    return jax.shard_map(
        per_device,
        mesh=mesh,
        in_specs=(P("inp", "tm"), P()),
        out_specs=P("tm", None, "inp", None),
        check_vma=False,
    )
```

```python
import functools
import math

import jax
import jax.numpy as jnp
import numpy as np
from jax import lax
from jax.experimental import pallas as pl
from jax.experimental.pallas import tpu as pltpu
from jax.sharding import PartitionSpec as P

MESH = pl.DeviceIdType.MESH
HEAD = 4
MIDDLE = 32
LAST = 32
TAIL = 8
OUTER = 1
INNER = 8
LATE = 8
SOON = 2
RING = 12
LANES = 128


def each(first, end, body):
    def step(d, carry):
        body(d)
        return carry

    lax.fori_loop(first, end, step, 0)


def across(me, mask, n):
    if n & (n - 1):
        return lax.rem(me + mask, n), lax.rem(me + n - mask, n)
    peer, bit = me, 1
    while bit < n:
        flip = lax.rem(mask // bit, 2)
        peer = peer + flip * bit * (1 - 2 * lax.rem(me // bit, 2))
        bit *= 2
    return peer, peer


def plan(ch_dev):
    head = max(ch_dev // HEAD, 1)
    tail = max(ch_dev // TAIL, 1)
    big = math.gcd(max(ch_dev // MIDDLE, 1), ch_dev - head - tail)
    per = math.gcd(max(ch_dev // LAST, 1), tail)
    bigs = (ch_dev - head - tail) // big
    return head, big, bigs, per, 1 + bigs + tail // per


def correlator(
    n_inp, n_tm, scale, x, weights, table_hbm, held,
    xb, halo, table, low, high, turn, spec, recv, part, got,
    x_sem, table_sem, halo_sem, send_sem, recv_sem, put_sem, got_sem,
):
    me = lax.axis_index("inp")
    seg = lax.axis_index("tm")
    ch_dev, _, _, in_dev, count = recv.shape
    groups, _, _, frame = halo.shape
    rim = halo.shape[1]
    pack = xb.shape[1]
    block = xb.shape[2] - rim
    width = pack * 8
    half = frame // 2
    fold = ch_dev // 2
    inputs = n_inp * in_dev
    rows = inputs // n_tm
    head, big, bigs, per, chunks = plan(ch_dev)
    in_units = in_dev // width
    s_units = count // block
    units = in_units * s_units

    barrier = pltpu.get_barrier_semaphore()
    for d in range(1, n_inp):
        pl.semaphore_signal(
            barrier, inc=1, device_id={"inp": lax.rem(me + d, n_inp)}, device_id_type=MESH
        )
    for d in range(1, n_tm):
        pl.semaphore_signal(
            barrier, inc=1, device_id={"tm": lax.rem(seg + d, n_tm)}, device_id_type=MESH
        )

    def place(u):
        return lax.rem(u, in_units), lax.rem(u // in_units + 1, s_units)

    def inner_load(u):
        g, s = place(u)
        slot = lax.rem(u, 2)
        return pltpu.make_async_copy(
            x.at[pl.ds(g * pack, pack), pl.ds(s * block - rim, block + rim)],
            xb.at[slot], x_sem.at[slot],
        )

    def first_load(u):
        g, _ = place(u)
        slot = lax.rem(u, 2)
        return pltpu.make_async_copy(
            x.at[pl.ds(g * pack, pack), pl.ds(0, block)],
            xb.at[slot, :, pl.ds(rim, block)], x_sem.at[slot],
        )

    def load(u, act):
        _, s = place(u)

        @pl.when(s > 0)
        def _():
            act(inner_load(u))

        @pl.when(s == 0)
        def _():
            act(first_load(u))

    def rim_copy():
        return pltpu.make_async_remote_copy(
            src_ref=x.at[:, pl.ds(count - rim, rim)],
            dst_ref=halo,
            send_sem=halo_sem.at[0],
            recv_sem=halo_sem.at[1],
            device_id={"tm": lax.rem(seg + 1, n_tm)},
            device_id_type=MESH,
        )

    table_copy = pltpu.make_async_copy(table_hbm, table, table_sem.at[0])
    load(0, lambda copy: copy.start())
    table_copy.start()

    def own_head():
        return pltpu.make_async_copy(
            spec.at[me, pl.ds(0, head)], recv.at[pl.ds(0, head), :, me], recv_sem.at[0]
        )

    def whole_chunk(c):
        return pl.ds(head + (c - 1) * big, big)

    def small_chunk(c):
        return pl.ds(head + bigs * big + (c - 1 - bigs) * per, per)

    def own_copy(c, chunk):
        return pltpu.make_async_copy(
            spec.at[me, chunk], recv.at[chunk, :, me], recv_sem.at[c]
        )

    def remote(mask, c, src, dst):
        return pltpu.make_async_remote_copy(
            src_ref=src,
            dst_ref=dst,
            send_sem=send_sem.at[0],
            recv_sem=recv_sem.at[c],
            device_id={"inp": across(me, mask, n_inp)[0]},
            device_id_type=MESH,
        )

    def unit_copy(u, mask):
        g, s = place(u)
        peer = across(me, mask, n_inp)[0]
        at = pl.ds(pl.multiple_of(g * width, width), width)
        span = pl.ds(pl.multiple_of(s * block, block), block)
        first = pl.ds(0, head)
        return remote(
            mask, 0, spec.at[peer, first, :, at, span], recv.at[first, :, me, at, span]
        )

    def take(c, chunk):
        pltpu.make_async_copy(recv.at[chunk], recv.at[chunk], recv_sem.at[c]).wait()

    def sent():
        most = spec.at[pl.ds(0, n_inp - 1)]
        pltpu.make_async_copy(most, most, send_sem.at[0]).wait()

    def chunk_copy(c, mask, chunk):
        peer = across(me, mask, n_inp)[0]
        return remote(mask, c, spec.at[peer, chunk], recv.at[chunk, :, me])

    def send_chunk(c, chunk):
        own_copy(c, chunk).start()
        each(0, n_inp - 1, lambda k: chunk_copy(c, n_inp - 1 - k, chunk).start())

    def send(c):
        @pl.when(c <= bigs)
        def _():
            send_chunk(c, whole_chunk(c))

        @pl.when(c > bigs)
        def _():
            send_chunk(c, small_chunk(c))

    def filter_unit(u):
        slot = lax.rem(u, 2)
        step = 8

        def some(k):
            g = k // (block // step)
            s = lax.rem(k, block // step) * step
            to = pl.ds(pl.multiple_of((g * block + s) * 8, step * 8), step * 8)
            for t in range(half // LANES):
                sides = []
                for first in (t * LANES, half + t * LANES):
                    lane = slice(first, first + LANES)
                    frames = xb[slot, g, pl.ds(s, step + rim), :, lane].astype(jnp.float32)
                    total = weights[0:1, lane][None] * frames[0:step]
                    for tap in range(1, rim + 1):
                        total = total + weights[tap : tap + 1, lane][None] * frames[tap : tap + step]
                    sides.append(total.reshape(step * 8, LANES))
                low[t, to] = sides[0] + sides[1]
                high[t, to] = sides[0] - sides[1]

        each(0, pack * (block // step), some)

    def transform(folded, odd):
        def pair(k):
            two = []
            for i in (2 * k, 2 * k + 1):
                at = (i // 8) * (block * 8) + lax.rem(i, 8)
                two.append(
                    jnp.concatenate(
                        [folded[t, pl.ds(at, block, stride=8), :] for t in range(half // LANES)],
                        axis=1,
                    )
                )
            value = jnp.concatenate(two, axis=0)
            top = value.astype(jnp.bfloat16)
            rest = (value - top.astype(jnp.float32)).astype(jnp.bfloat16)
            side = lax.dot_general(
                table[odd],
                jnp.concatenate([top, top, rest], axis=1),
                (((1,), (1,)), ((), ())),
                preferred_element_type=jnp.float32,
            )
            for n in range(2):
                turn[pl.ds(2 * k + n, half, stride=width), :] = side[:, n * block : (n + 1) * block]

        def several(k):
            for n in range(together):
                pair(together * k + n)

        pairs = width // 2
        together = math.gcd(pairs, 4)
        each(0, pairs // together, several)

    def spread(u, odd):
        g, s = place(u)
        at = pl.ds(pl.multiple_of(g * width, width), width)
        span = pl.ds(pl.multiple_of(s * block, block), block)
        lot = math.gcd(fold, 8)
        lots = fold // lot
        size = lot * 2 * width

        def some(k):
            rows_in = turn[pl.ds(pl.multiple_of(k * size, size), size), :]
            to = pl.ds(odd * fold + lax.rem(k, lots) * lot, lot)
            spec[k // lots, to, :, at, span] = rows_in.astype(jnp.bfloat16).reshape(
                lot, 2, width, block
            )

        each(0, n_inp * lots, some)

    def unit(u):
        @pl.when(u + 1 < units)
        def _():
            load(u + 1, lambda copy: copy.start())

        load(u, lambda copy: copy.wait())
        g, s = place(u)

        @pl.when(s == 0)
        def _():
            @pl.when(jnp.logical_and(seg > 0, u == units - in_units))
            def _():
                rim_copy().wait_recv()

            @pl.when(jnp.logical_and(seg == 0, u == units - in_units))
            def _():
                halo[...] = jnp.zeros_like(halo)

            xb[lax.rem(u, 2), :, 0:rim] = halo[pl.ds(g * pack, pack)]

        filter_unit(u)

        @pl.when(u == 0)
        def _():
            table_copy.wait()

        transform(low, 0)
        spread(u, 0)

        @pl.when(u == 0)
        def _():
            pl.semaphore_wait(barrier, n_inp - 1 + n_tm - 1)

            @pl.when(seg + 1 < n_tm)
            def _():
                rim_copy().start()

        each(0, n_inp - 1, lambda k: unit_copy(u, n_inp - 1 - k).start())
        transform(high, 1)
        spread(u, 1)

    each(0, units, unit)
    own_head().start()

    @pl.when(seg + 1 < n_tm)
    def _():
        rim_copy().wait_send()

    def sum_copy(g, d):
        peer = lax.rem(seg + d, n_tm)
        return pltpu.make_async_remote_copy(
            src_ref=part.at[lax.rem(g, RING), peer],
            dst_ref=got.at[d - 1, g],
            send_sem=put_sem.at[lax.rem(g, RING)],
            recv_sem=got_sem.at[g],
            device_id={"tm": peer},
            device_id_type=MESH,
        )

    def side(ch, p):
        value = recv[ch, p]
        if in_dev % 16 == 0:
            return value.reshape(inputs, count)
        return value.astype(jnp.float32).reshape(inputs, count).astype(jnp.bfloat16)

    def correlate(ch):
        real = side(ch, 0)
        imag = side(ch, 1)
        a = jnp.concatenate([real, imag], axis=1)
        b = jnp.concatenate([imag, -real], axis=1)
        for p, left in ((0, a), (1, b)):
            product = lax.dot_general(
                left, a, (((1,), (1,)), ((), ())), preferred_element_type=jnp.float32
            )
            for q in range(n_tm):
                part[lax.rem(ch, RING), q, p] = product[q * rows : (q + 1) * rows]

    def put(g):
        slot = lax.rem(g, RING)
        summed = part.at[slot, pl.ds(0, n_tm - 1)]
        pltpu.make_async_copy(summed, summed, put_sem.at[slot]).wait()

    def finish(g):
        summed = got.at[:, g]
        pltpu.make_async_copy(summed, summed, got_sem.at[g]).wait()
        ch = lax.rem(g, fold) * 2 + g // fold
        for p in range(2):
            total = part[lax.rem(g, RING), seg, p]
            for d in range(1, n_tm):
                total = total + got[d - 1, g, p]
            total = total * scale
            for t in range(inputs // LANES):
                at = pl.ds(p * ch_dev + ch, rows, stride=2 * ch_dev)
                held[t, at, :] = total[:, t * LANES : (t + 1) * LANES]

    def done(g):
        early = g + 1 - LATE
        late = ch_dev - SOON - 2 * (ch_dev - 1 - g)
        return jnp.maximum(jnp.maximum(early, late), 0)

    def channel(g):
        @pl.when(g >= RING)
        def _():
            put(g - RING)

        correlate(g)
        each(1, n_tm, lambda d: sum_copy(g, d).start())

        each(done(g - 1), done(g), finish)

    ring = me // max(n_inp // 4, 1)
    ahead = jnp.where(jnp.logical_and(ring > 0, ring < 3), INNER, OUTER)
    each(1, jnp.minimum(ahead, chunks), send)
    take(0, pl.ds(0, head))
    each(0, head, channel)

    def step(c):
        @pl.when(c + ahead - 1 < chunks)
        def _():
            send(c + ahead - 1)

        @pl.when(c <= bigs)
        def _():
            take(c, whole_chunk(c))

        @pl.when(c > bigs)
        def _():
            take(c, small_chunk(c))

        first = jnp.where(
            c <= bigs, head + (c - 1) * big, head + bigs * big + (c - 1 - bigs) * per
        )
        each(0, jnp.where(c <= bigs, big, per), lambda k: channel(first + k))

    each(1, chunks, step)
    each(done(ch_dev - 1), ch_dev, finish)
    sent()
    each(
        max(ch_dev - RING, 0),
        ch_dev,
        put,
    )


def deliver(held, out, sem):
    copies = [
        pltpu.make_async_copy(held.at[t], out.at[:, pl.ds(t * LANES, LANES)], sem.at[t])
        for t in range(held.shape[0])
    ]
    for copy in copies:
        copy.start()
    for copy in copies:
        copy.wait()


def tables(frame):
    fold = frame // 2
    sides = []
    for odd in (0, 1):
        column = np.arange(fold)
        channel = column // 2 * 2 + odd
        phase = np.arange(fold)[:, None] * channel[None, :] % frame
        angle = phase * (2.0 * math.pi / frame)
        whole = np.where(column % 2 == 0, np.cos(angle), -np.sin(angle)) * frame ** (-0.5)
        whole = whole.T.astype(np.float32)
        top = whole.astype(jnp.bfloat16)
        rest = (whole - top.astype(np.float32)).astype(jnp.bfloat16)
        sides.append(np.concatenate([top, rest, top], axis=1))
    return np.stack(sides)


def per_device(samples, tap_weights):
    in_dev = samples.shape[0]
    taps, frame = tap_weights.shape
    rim = taps - 1
    count = samples.shape[1] // frame
    n_inp = lax.axis_size("inp")
    n_tm = lax.axis_size("tm")
    ch_dev = frame // 2 // n_inp
    inputs = n_inp * in_dev
    rows = inputs // n_tm
    groups = in_dev // 8
    pack = math.gcd(groups, 2)
    block = LANES
    chunks = plan(ch_dev)[-1]
    scale = 1.0 / math.sqrt(count * n_tm)
    tiles = inputs // LANES
    frames = samples.reshape(groups, 8, count, frame).transpose(0, 2, 1, 3)
    mine = pl.pallas_call(
        functools.partial(correlator, n_inp, n_tm, scale),
        out_shape=pltpu.VMEM((tiles, rows * 2 * ch_dev, LANES), jnp.float32),
        in_specs=[
            pl.BlockSpec(memory_space=pltpu.HBM),
            pl.BlockSpec(memory_space=pltpu.VMEM),
            pl.BlockSpec(memory_space=pltpu.HBM),
        ],
        out_specs=pl.BlockSpec(memory_space=pltpu.VMEM),
        scratch_shapes=[
            pltpu.VMEM((2, pack, block + rim, 8, frame), jnp.bfloat16),
            pltpu.VMEM((groups, rim, 8, frame), jnp.bfloat16),
            pltpu.VMEM((2, frame // 2, 3 * (frame // 2)), jnp.bfloat16),
            pltpu.VMEM((frame // 2 // LANES, pack * block * 8, LANES), jnp.float32),
            pltpu.VMEM((frame // 2 // LANES, pack * block * 8, LANES), jnp.float32),
            pltpu.VMEM((frame // 2 * pack * 8, block), jnp.float32),
            pltpu.VMEM((n_inp, ch_dev, 2, in_dev, count), jnp.bfloat16),
            pltpu.VMEM((ch_dev, 2, n_inp, in_dev, count), jnp.bfloat16),
            pltpu.VMEM((RING, n_tm, 2, rows, inputs), jnp.float32),
            pltpu.VMEM((n_tm - 1, ch_dev, 2, rows, inputs), jnp.float32),
            pltpu.SemaphoreType.DMA((2,)),
            pltpu.SemaphoreType.DMA((1,)),
            pltpu.SemaphoreType.DMA((2,)),
            pltpu.SemaphoreType.DMA((1,)),
            pltpu.SemaphoreType.DMA((chunks,)),
            pltpu.SemaphoreType.DMA((RING,)),
            pltpu.SemaphoreType.DMA((ch_dev,)),
        ],
        compiler_params=pltpu.CompilerParams(
            collective_id=0, has_side_effects=True, vmem_limit_bytes=58 << 20
        ),
    )(frames, tap_weights, jnp.asarray(tables(frame)))
    whole = pl.pallas_call(
        deliver,
        out_shape=jax.ShapeDtypeStruct((rows * 2 * ch_dev, inputs), jnp.float32),
        in_specs=[pl.BlockSpec(memory_space=pltpu.VMEM)],
        out_specs=pl.BlockSpec(memory_space=pltpu.HBM),
        scratch_shapes=[pltpu.SemaphoreType.DMA((tiles,))],
        compiler_params=pltpu.CompilerParams(vmem_limit_bytes=8 << 20),
    )(pltpu.with_memory_space_constraint(mine, pltpu.VMEM))
    return whole.reshape(rows, 2, ch_dev, inputs)


def solution(mesh):
    return jax.shard_map(
        per_device,
        mesh=mesh,
        in_specs=(P("inp", "tm"), P()),
        out_specs=P("tm", None, "inp", None),
        check_vma=False,
    )
```

```python
import functools
import math

import jax
import jax.numpy as jnp
import numpy as np
from jax import lax
from jax.experimental import pallas as pl
from jax.experimental.pallas import tpu as pltpu
from jax.sharding import PartitionSpec as P

MESH = pl.DeviceIdType.MESH
HEAD = 4
STEPS = 32
OUTER = 1
INNER = 8
LATE = 8
SOON = 2
RING = 12
LANES = 128
PIECES = 1


def each(first, end, body):
    def step(d, carry):
        body(d)
        return carry

    lax.fori_loop(first, end, step, 0)


def across(me, mask, n):
    if n & (n - 1):
        return lax.rem(me + mask, n), lax.rem(me + n - mask, n)
    peer, bit = me, 1
    while bit < n:
        flip = lax.rem(mask // bit, 2)
        peer = peer + flip * bit * (1 - 2 * lax.rem(me // bit, 2))
        bit *= 2
    return peer, peer


def plan(ch_dev):
    head = max(ch_dev // HEAD, 1)
    per = math.gcd(max(ch_dev // STEPS, 1), ch_dev - head)
    return head, per, 1 + (ch_dev - head) // per


def correlator(
    n_inp, n_tm, scale, x, weights_hbm, table_hbm, held,
    weights, xb, halo, table, low, high, turn, spec, recv, part, got,
    weights_sem, x_sem, table_sem, halo_sem, send_sem, recv_sem, put_sem, got_sem,
):
    me = lax.axis_index("inp")
    seg = lax.axis_index("tm")
    ch_dev, _, _, in_dev, count = recv.shape
    groups, _, _, frame = halo.shape
    rim = halo.shape[1]
    pack = xb.shape[1]
    block = xb.shape[2] - rim
    width = pack * 8
    half = frame // 2
    fold = ch_dev // 2
    inputs = n_inp * in_dev
    rows = inputs // n_tm
    head, per, chunks = plan(ch_dev)
    in_units = in_dev // width
    s_units = count // block
    units = in_units * s_units

    def place(u):
        return lax.rem(u, in_units), lax.rem(u // in_units + 1, s_units)

    def inner_load(u, n):
        g, s = place(u)
        slot = lax.rem(u, 2)
        return pltpu.make_async_copy(
            x.at[g * pack + n, pl.ds(s * block - rim, block + rim)],
            xb.at[slot, n], x_sem.at[slot, n],
        )

    def first_load(u, n):
        g, _ = place(u)
        slot = lax.rem(u, 2)
        return pltpu.make_async_copy(
            x.at[g * pack + n, pl.ds(0, block)],
            xb.at[slot, n, pl.ds(rim, block)], x_sem.at[slot, n],
        )

    def load(u, n, act):
        _, s = place(u)

        @pl.when(s > 0)
        def _():
            act(inner_load(u, n))

        @pl.when(s == 0)
        def _():
            act(first_load(u, n))

    def load_all(u):
        for n in range(pack):
            load(u, n, lambda copy: copy.start())

    def rim_copy():
        return pltpu.make_async_remote_copy(
            src_ref=x.at[:, pl.ds(count - rim, rim)],
            dst_ref=halo,
            send_sem=halo_sem.at[0],
            recv_sem=halo_sem.at[1],
            device_id={"tm": lax.rem(seg + 1, n_tm)},
            device_id_type=MESH,
        )

    weights_copy = pltpu.make_async_copy(weights_hbm, weights, weights_sem.at[0])
    weights_copy.start()
    load_all(0)
    barrier = pltpu.get_barrier_semaphore()
    for d in range(1, n_inp):
        pl.semaphore_signal(
            barrier, inc=1, device_id={"inp": lax.rem(me + d, n_inp)}, device_id_type=MESH
        )
    for d in range(1, n_tm):
        pl.semaphore_signal(
            barrier, inc=1, device_id={"tm": lax.rem(seg + d, n_tm)}, device_id_type=MESH
        )

    table_copy = pltpu.make_async_copy(table_hbm, table, table_sem.at[0])
    table_copy.start()

    def own_head():
        return pltpu.make_async_copy(
            spec.at[me, pl.ds(0, head)], recv.at[pl.ds(0, head), :, me], recv_sem.at[0]
        )

    def channels(c):
        return pl.ds(head + (c - 1) * per, per)

    def own_copy(c):
        return pltpu.make_async_copy(
            spec.at[me, channels(c)], recv.at[channels(c), :, me], recv_sem.at[c]
        )

    def remote(mask, c, src, dst):
        return pltpu.make_async_remote_copy(
            src_ref=src,
            dst_ref=dst,
            send_sem=send_sem.at[0],
            recv_sem=recv_sem.at[c],
            device_id={"inp": across(me, mask, n_inp)[0]},
            device_id_type=MESH,
        )

    def unit_copy(u, mask):
        g, s = place(u)
        peer = across(me, mask, n_inp)[0]
        at = pl.ds(pl.multiple_of(g * width, width), width)
        span = pl.ds(pl.multiple_of(s * block, block), block)
        first = pl.ds(0, head)
        return remote(
            mask, 0, spec.at[peer, first, :, at, span], recv.at[first, :, me, at, span]
        )

    def take(c, chunk):
        pltpu.make_async_copy(recv.at[chunk], recv.at[chunk], recv_sem.at[c]).wait()

    def sent():
        most = spec.at[pl.ds(0, n_inp - 1)]
        pltpu.make_async_copy(most, most, send_sem.at[0]).wait()

    def chunk_copy(c, mask):
        peer = across(me, mask, n_inp)[0]
        return remote(mask, c, spec.at[peer, channels(c)], recv.at[channels(c), :, me])

    def order(k):
        if n_inp & (n_inp - 1) or n_inp < 4:
            return n_inp - 1 - k
        lot = n_inp // 4
        far = n_inp - 1 - 2 * lax.rem(k, lot) - lax.rem(k // lot + me, 2)
        return jnp.where(k < 2 * lot, far, n_inp - 1 - k)

    def send(c):
        own_copy(c).start()
        each(0, n_inp - 1, lambda k: chunk_copy(c, order(k)).start())

    def filter_unit(u):
        slot = lax.rem(u, 2)
        step = 8

        def some(g, k):
            s = k * step
            to = pl.ds(pl.multiple_of((g * block + s) * 8, step * 8), step * 8)
            for t in range(half // LANES):
                sides = []
                for first in (t * LANES, half + t * LANES):
                    lane = slice(first, first + LANES)
                    frames = xb[slot, g, pl.ds(s, step + rim), :, lane].astype(jnp.float32)
                    total = weights[0:1, lane][None] * frames[0:step]
                    for tap in range(1, rim + 1):
                        total = total + weights[tap : tap + 1, lane][None] * frames[tap : tap + step]
                    sides.append(total.reshape(step * 8, LANES))
                low[t, to] = sides[0] + sides[1]
                high[t, to] = sides[0] - sides[1]

        for g in range(pack):
            load(u, g, lambda copy: copy.wait())
            each(0, block // step, functools.partial(some, g))

    def transform(folded, odd, start, size):
        def pair(k):
            two = []
            for i in (2 * k, 2 * k + 1):
                at = (i // 8) * (block * 8) + lax.rem(i, 8)
                two.append(
                    jnp.concatenate(
                        [folded[t, pl.ds(at, block, stride=8), :] for t in range(half // LANES)],
                        axis=1,
                    )
                )
            value = jnp.concatenate(two, axis=0)
            top = value.astype(jnp.bfloat16)
            rest = (value - top.astype(jnp.float32)).astype(jnp.bfloat16)
            side = lax.dot_general(
                table[odd, start : start + size],
                jnp.concatenate([top, top, rest], axis=1),
                (((1,), (1,)), ((), ())),
                preferred_element_type=jnp.float32,
            )
            for n in range(2):
                at = pl.ds(start * width + 2 * k + n, size, stride=width)
                turn[at, :] = side[:, n * block : (n + 1) * block]

        def several(k):
            for n in range(together):
                pair(together * k + n)

        pairs = width // 2
        together = math.gcd(pairs, 8)
        each(0, pairs // together, several)

    def spread(u, odd, start, size):
        g, s = place(u)
        at = pl.ds(pl.multiple_of(g * width, width), width)
        span = pl.ds(pl.multiple_of(s * block, block), block)
        lot = size // (2 * n_inp)
        to = pl.ds(odd * fold + start // (2 * n_inp), lot)
        length = lot * 2 * width

        def some(k):
            first = start * width + k * length
            rows_in = turn[pl.ds(pl.multiple_of(first, length), length), :]
            spec[k, to, :, at, span] = rows_in.astype(jnp.bfloat16).reshape(lot, 2, width, block)

        each(0, n_inp, some)

    front = 2 * n_inp * min(head, fold)

    def spread_all(u, odd):
        spread(u, odd, 0, front)
        if front < half:
            spread(u, odd, front, half - front)

    def unit(u):
        @pl.when(u + 1 < units)
        def _():
            load_all(u + 1)

        g, s = place(u)

        @pl.when(s == 0)
        def _():
            @pl.when(jnp.logical_and(seg > 0, u == units - in_units))
            def _():
                rim_copy().wait_recv()

            @pl.when(jnp.logical_and(seg == 0, u == units - in_units))
            def _():
                halo[...] = jnp.zeros_like(halo)

            xb[lax.rem(u, 2), :, 0:rim] = halo[pl.ds(g * pack, pack)]

        @pl.when(u == 0)
        def _():
            weights_copy.wait()

        filter_unit(u)

        @pl.when(u == 0)
        def _():
            table_copy.wait()

        @pl.when(u == 0)
        def _():
            transform(low, 0, 0, front)
            spread(u, 0, 0, front)
            pl.semaphore_wait(barrier, n_inp - 1 + n_tm - 1)

            @pl.when(seg + 1 < n_tm)
            def _():
                rim_copy().start()

        @pl.when(u > 0)
        def _():
            transform(low, 0, 0, half)
            spread_all(u, 0)

        each(0, n_inp - 1, lambda k: unit_copy(u, order(k)).start())

        @pl.when(u == 0)
        def _():
            if front < half:
                transform(low, 0, front, half - front)
                spread(u, 0, front, half - front)

        transform(high, 1, 0, half)
        spread_all(u, 1)

    each(0, units, unit)
    own_head().start()

    @pl.when(seg + 1 < n_tm)
    def _():
        rim_copy().wait_send()

    def sum_copy(g, mask):
        peer = across(seg, mask, n_tm)[0]
        return pltpu.make_async_remote_copy(
            src_ref=part.at[lax.rem(g, RING), peer],
            dst_ref=got.at[mask - 1, g],
            send_sem=put_sem.at[lax.rem(g, RING)],
            recv_sem=got_sem.at[g],
            device_id={"tm": peer},
            device_id_type=MESH,
        )

    def side(ch, p):
        value = recv[ch, p]
        if in_dev % 16 == 0:
            return value.reshape(inputs, count)
        return value.astype(jnp.float32).reshape(inputs, count).astype(jnp.bfloat16)

    def correlate(ch):
        real = side(ch, 0)
        imag = side(ch, 1)
        a = jnp.concatenate([real, imag], axis=1)
        b = jnp.concatenate([imag, -real], axis=1)
        for p, left in ((0, a), (1, b)):
            product = lax.dot_general(
                left, a, (((1,), (1,)), ((), ())), preferred_element_type=jnp.float32
            )
            for q in range(n_tm):
                part[lax.rem(ch, RING), q, p] = product[q * rows : (q + 1) * rows]

    def put(g):
        slot = lax.rem(g, RING)
        summed = part.at[slot, pl.ds(0, n_tm - 1)]
        pltpu.make_async_copy(summed, summed, put_sem.at[slot]).wait()

    def finish(g):
        summed = got.at[:, g]
        pltpu.make_async_copy(summed, summed, got_sem.at[g]).wait()
        ch = lax.rem(g, fold) * 2 + g // fold
        for p in range(2):
            total = part[lax.rem(g, RING), seg, p]
            for d in range(1, n_tm):
                total = total + got[d - 1, g, p]
            total = total * scale
            for t in range(inputs // LANES):
                at = pl.ds(p * ch_dev + ch, rows, stride=2 * ch_dev)
                held[t, at, :] = total[:, t * LANES : (t + 1) * LANES]

    def done(g):
        early = g + 1 - LATE
        late = ch_dev - SOON - 2 * (ch_dev - 1 - g)
        return jnp.maximum(jnp.maximum(early, late), 0)

    def channel(g):
        @pl.when(g >= RING)
        def _():
            put(g - RING)

        correlate(g)
        each(1, n_tm, lambda d: sum_copy(g, n_tm - d).start())

        each(done(g - 1), done(g), finish)

    ring = me // max(n_inp // 4, 1)
    ahead = jnp.where(jnp.logical_and(ring > 0, ring < 3), INNER, OUTER)
    each(1, jnp.minimum(ahead, chunks), send)
    take(0, pl.ds(0, head))
    each(0, head, channel)

    def step(c):
        @pl.when(c + ahead - 1 < chunks)
        def _():
            send(c + ahead - 1)

        take(c, channels(c))
        each(0, per, lambda k: channel(head + (c - 1) * per + k))

    each(1, chunks, step)
    each(done(ch_dev - 1), ch_dev, finish)
    sent()
    each(
        max(ch_dev - RING, 0),
        ch_dev,
        put,
    )


def deliver(held, out, sem):
    tiles, length, _ = held.shape
    piece = length // PIECES
    copies = [
        pltpu.make_async_copy(
            held.at[t, pl.ds(n * piece, piece)],
            out.at[pl.ds(n * piece, piece), pl.ds(t * LANES, LANES)],
            sem.at[t * PIECES + n],
        )
        for n in range(PIECES)
        for t in range(tiles)
    ]
    for copy in copies:
        copy.start()
    for copy in copies:
        copy.wait()


def tables(frame, n_inp, head):
    fold = frame // 2
    columns = np.arange(fold).reshape(n_inp, fold // (2 * n_inp), 2)
    parts = [columns[:, :head].reshape(-1), columns[:, head:].reshape(-1)]
    order = np.concatenate(parts)
    sides = []
    for odd in (0, 1):
        column = np.arange(fold)
        channel = column // 2 * 2 + odd
        phase = np.arange(fold)[:, None] * channel[None, :] % frame
        angle = phase * (2.0 * math.pi / frame)
        whole = np.where(column % 2 == 0, np.cos(angle), -np.sin(angle)) * frame ** (-0.5)
        whole = whole.T[order].astype(np.float32)
        top = whole.astype(jnp.bfloat16)
        rest = (whole - top.astype(np.float32)).astype(jnp.bfloat16)
        sides.append(np.concatenate([top, rest, top], axis=1))
    return np.stack(sides)


def per_device(samples, tap_weights):
    in_dev = samples.shape[0]
    taps, frame = tap_weights.shape
    rim = taps - 1
    count = samples.shape[1] // frame
    n_inp = lax.axis_size("inp")
    n_tm = lax.axis_size("tm")
    ch_dev = frame // 2 // n_inp
    inputs = n_inp * in_dev
    rows = inputs // n_tm
    groups = in_dev // 8
    pack = math.gcd(groups, 2)
    block = LANES
    chunks = plan(ch_dev)[-1]
    scale = 1.0 / math.sqrt(count * n_tm)
    tiles = inputs // LANES
    frames = samples.reshape(groups, 8, count, frame).transpose(0, 2, 1, 3)
    mine = pl.pallas_call(
        functools.partial(correlator, n_inp, n_tm, scale),
        out_shape=pltpu.VMEM((tiles, rows * 2 * ch_dev, LANES), jnp.float32),
        in_specs=[
            pl.BlockSpec(memory_space=pltpu.HBM),
            pl.BlockSpec(memory_space=pltpu.HBM),
            pl.BlockSpec(memory_space=pltpu.HBM),
        ],
        out_specs=pl.BlockSpec(memory_space=pltpu.VMEM),
        scratch_shapes=[
            pltpu.VMEM((taps, frame), jnp.float32),
            pltpu.VMEM((2, pack, block + rim, 8, frame), jnp.bfloat16),
            pltpu.VMEM((groups, rim, 8, frame), jnp.bfloat16),
            pltpu.VMEM((2, frame // 2, 3 * (frame // 2)), jnp.bfloat16),
            pltpu.VMEM((frame // 2 // LANES, pack * block * 8, LANES), jnp.float32),
            pltpu.VMEM((frame // 2 // LANES, pack * block * 8, LANES), jnp.float32),
            pltpu.VMEM((frame // 2 * pack * 8, block), jnp.float32),
            pltpu.VMEM((n_inp, ch_dev, 2, in_dev, count), jnp.bfloat16),
            pltpu.VMEM((ch_dev, 2, n_inp, in_dev, count), jnp.bfloat16),
            pltpu.VMEM((RING, n_tm, 2, rows, inputs), jnp.float32),
            pltpu.VMEM((n_tm - 1, ch_dev, 2, rows, inputs), jnp.float32),
            pltpu.SemaphoreType.DMA((1,)),
            pltpu.SemaphoreType.DMA((2, pack)),
            pltpu.SemaphoreType.DMA((1,)),
            pltpu.SemaphoreType.DMA((2,)),
            pltpu.SemaphoreType.DMA((1,)),
            pltpu.SemaphoreType.DMA((chunks,)),
            pltpu.SemaphoreType.DMA((RING,)),
            pltpu.SemaphoreType.DMA((ch_dev,)),
        ],
        compiler_params=pltpu.CompilerParams(
            collective_id=0, has_side_effects=True, vmem_limit_bytes=58 << 20
        ),
    )(frames, tap_weights, jnp.asarray(tables(frame, n_inp, plan(ch_dev)[0])))
    whole = pl.pallas_call(
        deliver,
        out_shape=jax.ShapeDtypeStruct((rows * 2 * ch_dev, inputs), jnp.float32),
        in_specs=[pl.BlockSpec(memory_space=pltpu.VMEM)],
        out_specs=pl.BlockSpec(memory_space=pltpu.HBM),
        scratch_shapes=[pltpu.SemaphoreType.DMA((tiles * PIECES,))],
        compiler_params=pltpu.CompilerParams(vmem_limit_bytes=8 << 20),
    )(pltpu.with_memory_space_constraint(mine, pltpu.VMEM))
    return whole.reshape(rows, 2, ch_dev, inputs)


def solution(mesh):
    return jax.shard_map(
        per_device,
        mesh=mesh,
        in_specs=(P("inp", "tm"), P()),
        out_specs=P("tm", None, "inp", None),
        check_vma=False,
    )
```

```python
import functools
import math

import jax
import jax.numpy as jnp
import numpy as np
from jax import lax
from jax.experimental import pallas as pl
from jax.experimental.pallas import tpu as pltpu
from jax.sharding import PartitionSpec as P

MESH = pl.DeviceIdType.MESH
HEAD = 4
STEPS = 32
OUTER = 1
INNER = 8
LATE = 8
SOON = 2
RING = 12
LANES = 128
PIECES = 1


def each(first, end, body):
    def step(d, carry):
        body(d)
        return carry

    lax.fori_loop(first, end, step, 0)


def across(me, mask, n):
    if n & (n - 1):
        return lax.rem(me + mask, n), lax.rem(me + n - mask, n)
    peer, bit = me, 1
    while bit < n:
        flip = lax.rem(mask // bit, 2)
        peer = peer + flip * bit * (1 - 2 * lax.rem(me // bit, 2))
        bit *= 2
    return peer, peer


def plan(ch_dev):
    head = max(ch_dev // HEAD, 1)
    per = math.gcd(max(ch_dev // STEPS, 1), ch_dev - head)
    return head, per, 1 + (ch_dev - head) // per


def correlator(
    n_inp, n_tm, scale, x, weights_hbm, table_hbm, held,
    weights, xb, halo, table, low, high, turn, spec, recv, part, got,
    weights_sem, x_sem, table_sem, halo_sem, send_sem, recv_sem, put_sem, got_sem,
):
    me = lax.axis_index("inp")
    seg = lax.axis_index("tm")
    ch_dev, _, _, in_dev, count = recv.shape
    groups, _, _, frame = halo.shape
    rim = halo.shape[1]
    pack = xb.shape[1]
    block = xb.shape[2] - rim
    width = pack * 8
    half = frame // 2
    fold = ch_dev // 2
    inputs = n_inp * in_dev
    rows = inputs // n_tm
    head, per, chunks = plan(ch_dev)
    in_units = in_dev // width
    s_units = count // block
    units = in_units * s_units

    def place(u):
        return lax.rem(u, in_units), lax.rem(u // in_units + 1, s_units)

    def inner_load(u, n):
        g, s = place(u)
        slot = lax.rem(u, 2)
        return pltpu.make_async_copy(
            x.at[g * pack + n, pl.ds(s * block - rim, block + rim)],
            xb.at[slot, n], x_sem.at[slot, n],
        )

    def first_load(u, n):
        g, _ = place(u)
        slot = lax.rem(u, 2)
        return pltpu.make_async_copy(
            x.at[g * pack + n, pl.ds(0, block)],
            xb.at[slot, n, pl.ds(rim, block)], x_sem.at[slot, n],
        )

    def load(u, n, act):
        _, s = place(u)

        @pl.when(s > 0)
        def _():
            act(inner_load(u, n))

        @pl.when(s == 0)
        def _():
            act(first_load(u, n))

    def load_all(u):
        for n in range(pack):
            load(u, n, lambda copy: copy.start())

    def rim_copy():
        return pltpu.make_async_remote_copy(
            src_ref=x.at[:, pl.ds(count - rim, rim)],
            dst_ref=halo,
            send_sem=halo_sem.at[0],
            recv_sem=halo_sem.at[1],
            device_id={"tm": lax.rem(seg + 1, n_tm)},
            device_id_type=MESH,
        )

    weights_copy = pltpu.make_async_copy(weights_hbm, weights, weights_sem.at[0])
    weights_copy.start()
    load_all(0)
    barrier = pltpu.get_barrier_semaphore()
    for d in range(1, n_inp):
        pl.semaphore_signal(
            barrier, inc=1, device_id={"inp": lax.rem(me + d, n_inp)}, device_id_type=MESH
        )
    for d in range(1, n_tm):
        pl.semaphore_signal(
            barrier, inc=1, device_id={"tm": lax.rem(seg + d, n_tm)}, device_id_type=MESH
        )

    table_copy = pltpu.make_async_copy(table_hbm, table, table_sem.at[0])
    table_copy.start()

    def own_head():
        return pltpu.make_async_copy(
            spec.at[me, pl.ds(0, head)], recv.at[pl.ds(0, head), :, me], recv_sem.at[0]
        )

    def channels(c):
        return pl.ds(head + (c - 1) * per, per)

    def own_copy(c):
        return pltpu.make_async_copy(
            spec.at[me, channels(c)], recv.at[channels(c), :, me], recv_sem.at[c]
        )

    def remote(mask, c, src, dst):
        return pltpu.make_async_remote_copy(
            src_ref=src,
            dst_ref=dst,
            send_sem=send_sem.at[0],
            recv_sem=recv_sem.at[c],
            device_id={"inp": across(me, mask, n_inp)[0]},
            device_id_type=MESH,
        )

    def unit_copy(u, mask):
        g, s = place(u)
        peer = across(me, mask, n_inp)[0]
        at = pl.ds(pl.multiple_of(g * width, width), width)
        span = pl.ds(pl.multiple_of(s * block, block), block)
        first = pl.ds(0, head)
        return remote(
            mask, 0, spec.at[peer, first, :, at, span], recv.at[first, :, me, at, span]
        )

    def take(c, chunk):
        pltpu.make_async_copy(recv.at[chunk], recv.at[chunk], recv_sem.at[c]).wait()

    def sent():
        most = spec.at[pl.ds(0, n_inp - 1)]
        pltpu.make_async_copy(most, most, send_sem.at[0]).wait()

    def chunk_copy(c, mask):
        peer = across(me, mask, n_inp)[0]
        return remote(mask, c, spec.at[peer, channels(c)], recv.at[channels(c), :, me])

    def order(k):
        if n_inp & (n_inp - 1) or n_inp < 4:
            return n_inp - 1 - k
        lot = n_inp // 4
        far = n_inp - 1 - 2 * lax.rem(k, lot) - lax.rem(k // lot + me, 2)
        return jnp.where(k < 2 * lot, far, n_inp - 1 - k)

    def send(c):
        own_copy(c).start()
        each(0, n_inp - 1, lambda k: chunk_copy(c, order(k)).start())

    def filter_unit(u):
        slot = lax.rem(u, 2)
        step = 8

        def some(g, k):
            s = k * step
            to = pl.ds(pl.multiple_of((g * block + s) * 8, step * 8), step * 8)
            for t in range(half // LANES):
                sides = []
                for first in (t * LANES, half + t * LANES):
                    lane = slice(first, first + LANES)
                    frames = xb[slot, g, pl.ds(s, step + rim), :, lane].astype(jnp.float32)
                    total = weights[0:1, lane][None] * frames[0:step]
                    for tap in range(1, rim + 1):
                        total = total + weights[tap : tap + 1, lane][None] * frames[tap : tap + step]
                    sides.append(total.reshape(step * 8, LANES))
                low[t, to] = sides[0] + sides[1]
                high[t, to] = sides[0] - sides[1]

        for g in range(pack):
            load(u, g, lambda copy: copy.wait())
            each(0, block // step, functools.partial(some, g))

    def transform(folded, odd, start, size):
        def pair(k):
            two = []
            for i in (2 * k, 2 * k + 1):
                at = (i // 8) * (block * 8) + lax.rem(i, 8)
                two.append(
                    jnp.concatenate(
                        [folded[t, pl.ds(at, block, stride=8), :] for t in range(half // LANES)],
                        axis=1,
                    )
                )
            value = jnp.concatenate(two, axis=0)
            top = value.astype(jnp.bfloat16)
            rest = (value - top.astype(jnp.float32)).astype(jnp.bfloat16)
            side = lax.dot_general(
                table[odd, start : start + size],
                jnp.concatenate([top, top, rest], axis=1),
                (((1,), (1,)), ((), ())),
                preferred_element_type=jnp.float32,
            )
            for n in range(2):
                at = pl.ds(start * width + 2 * k + n, size, stride=width)
                turn[at, :] = side[:, n * block : (n + 1) * block]

        def several(k):
            for n in range(together):
                pair(together * k + n)

        pairs = width // 2
        together = math.gcd(pairs, 8)
        each(0, pairs // together, several)

    def spread(u, odd, start, size):
        g, s = place(u)
        at = pl.ds(pl.multiple_of(g * width, width), width)
        span = pl.ds(pl.multiple_of(s * block, block), block)
        lot = size // (2 * n_inp)
        to = pl.ds(odd * fold + start // (2 * n_inp), lot)
        length = lot * 2 * width

        def some(k):
            first = start * width + k * length
            rows_in = turn[pl.ds(pl.multiple_of(first, length), length), :]
            spec[k, to, :, at, span] = rows_in.astype(jnp.bfloat16).reshape(lot, 2, width, block)

        each(0, n_inp, some)

    front = 2 * n_inp * min(head, fold)

    def spread_all(u, odd):
        spread(u, odd, 0, front)
        if front < half:
            spread(u, odd, front, half - front)

    def unit(u):
        @pl.when(u + 1 < units)
        def _():
            load_all(u + 1)

        g, s = place(u)

        @pl.when(s == 0)
        def _():
            @pl.when(jnp.logical_and(seg > 0, u == units - in_units))
            def _():
                rim_copy().wait_recv()

            @pl.when(jnp.logical_and(seg == 0, u == units - in_units))
            def _():
                halo[...] = jnp.zeros_like(halo)

            xb[lax.rem(u, 2), :, 0:rim] = halo[pl.ds(g * pack, pack)]

        @pl.when(u == 0)
        def _():
            weights_copy.wait()

        filter_unit(u)

        @pl.when(u == 0)
        def _():
            table_copy.wait()

        @pl.when(u == 0)
        def _():
            transform(low, 0, 0, front)
            spread(u, 0, 0, front)
            pl.semaphore_wait(barrier, n_inp - 1 + n_tm - 1)

            @pl.when(seg + 1 < n_tm)
            def _():
                rim_copy().start()

        @pl.when(u > 0)
        def _():
            transform(low, 0, 0, half)
            spread_all(u, 0)

        each(0, n_inp - 1, lambda k: unit_copy(u, order(k)).start())

        @pl.when(u == 0)
        def _():
            if front < half:
                transform(low, 0, front, half - front)
                spread(u, 0, front, half - front)

        transform(high, 1, 0, half)
        spread_all(u, 1)

    each(0, units, unit)
    own_head().start()

    @pl.when(seg + 1 < n_tm)
    def _():
        rim_copy().wait_send()

    def sum_copy(g, p, mask):
        peer = across(seg, mask, n_tm)[0]
        return pltpu.make_async_remote_copy(
            src_ref=part.at[lax.rem(g, RING), peer, p],
            dst_ref=got.at[mask - 1, g, p],
            send_sem=put_sem.at[lax.rem(g, RING)],
            recv_sem=got_sem.at[g],
            device_id={"tm": peer},
            device_id_type=MESH,
        )

    def side(ch, p):
        value = recv[ch, p]
        if in_dev % 16 == 0:
            return value.reshape(inputs, count)
        return value.astype(jnp.float32).reshape(inputs, count).astype(jnp.bfloat16)

    def leave(ch, p, d):
        sum_copy(ch, p, n_tm - d).start()

    def correlate(ch):
        real = side(ch, 0)
        imag = side(ch, 1)
        a = jnp.concatenate([real, imag], axis=1)
        b = jnp.concatenate([imag, -real], axis=1)
        for p, left in ((0, a), (1, b)):
            product = lax.dot_general(
                left, a, (((1,), (1,)), ((), ())), preferred_element_type=jnp.float32
            )
            for q in range(n_tm):
                part[lax.rem(ch, RING), q, p] = product[q * rows : (q + 1) * rows]
            each(1, n_tm, functools.partial(leave, ch, p))

    def put(g):
        slot = lax.rem(g, RING)
        summed = part.at[slot, pl.ds(0, n_tm - 1)]
        pltpu.make_async_copy(summed, summed, put_sem.at[slot]).wait()

    def finish(g):
        summed = got.at[:, g]
        pltpu.make_async_copy(summed, summed, got_sem.at[g]).wait()
        ch = lax.rem(g, fold) * 2 + g // fold
        for p in range(2):
            total = part[lax.rem(g, RING), seg, p]
            for d in range(1, n_tm):
                total = total + got[d - 1, g, p]
            total = total * scale
            for t in range(inputs // LANES):
                at = pl.ds(p * ch_dev + ch, rows, stride=2 * ch_dev)
                held[t, at, :] = total[:, t * LANES : (t + 1) * LANES]

    def done(g):
        early = g + 1 - LATE
        late = ch_dev - SOON - 2 * (ch_dev - 1 - g)
        return jnp.maximum(jnp.maximum(early, late), 0)

    def channel(g):
        @pl.when(g >= RING)
        def _():
            put(g - RING)

        correlate(g)

        each(done(g - 1), done(g), finish)

    ring = me // max(n_inp // 4, 1)
    ahead = jnp.where(jnp.logical_and(ring > 0, ring < 3), INNER, OUTER)
    each(1, jnp.minimum(ahead, chunks), send)
    take(0, pl.ds(0, head))
    each(0, head, channel)

    def step(c):
        @pl.when(c + ahead - 1 < chunks)
        def _():
            send(c + ahead - 1)

        take(c, channels(c))
        each(0, per, lambda k: channel(head + (c - 1) * per + k))

    each(1, chunks, step)
    each(done(ch_dev - 1), ch_dev, finish)
    sent()
    each(
        max(ch_dev - RING, 0),
        ch_dev,
        put,
    )


def deliver(held, out, sem):
    tiles, length, _ = held.shape
    piece = length // PIECES
    copies = [
        pltpu.make_async_copy(
            held.at[t, pl.ds(n * piece, piece)],
            out.at[pl.ds(n * piece, piece), pl.ds(t * LANES, LANES)],
            sem.at[t * PIECES + n],
        )
        for n in range(PIECES)
        for t in range(tiles)
    ]
    for copy in copies:
        copy.start()
    for copy in copies:
        copy.wait()


def tables(frame, n_inp, head):
    fold = frame // 2
    columns = np.arange(fold).reshape(n_inp, fold // (2 * n_inp), 2)
    parts = [columns[:, :head].reshape(-1), columns[:, head:].reshape(-1)]
    order = np.concatenate(parts)
    sides = []
    for odd in (0, 1):
        column = np.arange(fold)
        channel = column // 2 * 2 + odd
        phase = np.arange(fold)[:, None] * channel[None, :] % frame
        angle = phase * (2.0 * math.pi / frame)
        whole = np.where(column % 2 == 0, np.cos(angle), -np.sin(angle)) * frame ** (-0.5)
        whole = whole.T[order].astype(np.float32)
        top = whole.astype(jnp.bfloat16)
        rest = (whole - top.astype(np.float32)).astype(jnp.bfloat16)
        sides.append(np.concatenate([top, rest, top], axis=1))
    return np.stack(sides)


def per_device(samples, tap_weights):
    in_dev = samples.shape[0]
    taps, frame = tap_weights.shape
    rim = taps - 1
    count = samples.shape[1] // frame
    n_inp = lax.axis_size("inp")
    n_tm = lax.axis_size("tm")
    ch_dev = frame // 2 // n_inp
    inputs = n_inp * in_dev
    rows = inputs // n_tm
    groups = in_dev // 8
    pack = math.gcd(groups, 2)
    block = LANES
    chunks = plan(ch_dev)[-1]
    scale = 1.0 / math.sqrt(count * n_tm)
    tiles = inputs // LANES
    frames = samples.reshape(groups, 8, count, frame).transpose(0, 2, 1, 3)
    mine = pl.pallas_call(
        functools.partial(correlator, n_inp, n_tm, scale),
        out_shape=pltpu.VMEM((tiles, rows * 2 * ch_dev, LANES), jnp.float32),
        in_specs=[
            pl.BlockSpec(memory_space=pltpu.HBM),
            pl.BlockSpec(memory_space=pltpu.HBM),
            pl.BlockSpec(memory_space=pltpu.HBM),
        ],
        out_specs=pl.BlockSpec(memory_space=pltpu.VMEM),
        scratch_shapes=[
            pltpu.VMEM((taps, frame), jnp.float32),
            pltpu.VMEM((2, pack, block + rim, 8, frame), jnp.bfloat16),
            pltpu.VMEM((groups, rim, 8, frame), jnp.bfloat16),
            pltpu.VMEM((2, frame // 2, 3 * (frame // 2)), jnp.bfloat16),
            pltpu.VMEM((frame // 2 // LANES, pack * block * 8, LANES), jnp.float32),
            pltpu.VMEM((frame // 2 // LANES, pack * block * 8, LANES), jnp.float32),
            pltpu.VMEM((frame // 2 * pack * 8, block), jnp.float32),
            pltpu.VMEM((n_inp, ch_dev, 2, in_dev, count), jnp.bfloat16),
            pltpu.VMEM((ch_dev, 2, n_inp, in_dev, count), jnp.bfloat16),
            pltpu.VMEM((RING, n_tm, 2, rows, inputs), jnp.float32),
            pltpu.VMEM((n_tm - 1, ch_dev, 2, rows, inputs), jnp.float32),
            pltpu.SemaphoreType.DMA((1,)),
            pltpu.SemaphoreType.DMA((2, pack)),
            pltpu.SemaphoreType.DMA((1,)),
            pltpu.SemaphoreType.DMA((2,)),
            pltpu.SemaphoreType.DMA((1,)),
            pltpu.SemaphoreType.DMA((chunks,)),
            pltpu.SemaphoreType.DMA((RING,)),
            pltpu.SemaphoreType.DMA((ch_dev,)),
        ],
        compiler_params=pltpu.CompilerParams(
            collective_id=0, has_side_effects=True, vmem_limit_bytes=58 << 20
        ),
    )(frames, tap_weights, jnp.asarray(tables(frame, n_inp, plan(ch_dev)[0])))
    whole = pl.pallas_call(
        deliver,
        out_shape=jax.ShapeDtypeStruct((rows * 2 * ch_dev, inputs), jnp.float32),
        in_specs=[pl.BlockSpec(memory_space=pltpu.VMEM)],
        out_specs=pl.BlockSpec(memory_space=pltpu.HBM),
        scratch_shapes=[pltpu.SemaphoreType.DMA((tiles * PIECES,))],
        compiler_params=pltpu.CompilerParams(vmem_limit_bytes=8 << 20),
    )(pltpu.with_memory_space_constraint(mine, pltpu.VMEM))
    return whole.reshape(rows, 2, ch_dev, inputs)


def solution(mesh):
    return jax.shard_map(
        per_device,
        mesh=mesh,
        in_specs=(P("inp", "tm"), P()),
        out_specs=P("tm", None, "inp", None),
        check_vma=False,
    )
```

```python
import functools
import math

import jax
import jax.numpy as jnp
import numpy as np
from jax import lax
from jax.experimental import pallas as pl
from jax.experimental.pallas import tpu as pltpu
from jax.sharding import PartitionSpec as P

MESH = pl.DeviceIdType.MESH
HEAD = 4
STEPS = 32
OUTER = 1
INNER = 3
LATE = 8
SOON = 2
RING = 12
LANES = 128
PIECES = 1


def each(first, end, body):
    def step(d, carry):
        body(d)
        return carry

    lax.fori_loop(first, end, step, 0)


def across(me, mask, n):
    if n & (n - 1):
        return lax.rem(me + mask, n), lax.rem(me + n - mask, n)
    peer, bit = me, 1
    while bit < n:
        flip = lax.rem(mask // bit, 2)
        peer = peer + flip * bit * (1 - 2 * lax.rem(me // bit, 2))
        bit *= 2
    return peer, peer


def plan(ch_dev):
    head = max(ch_dev // HEAD, 1)
    per = math.gcd(max(ch_dev // STEPS, 1), ch_dev - head)
    return head, per, 1 + (ch_dev - head) // per


def correlator(
    n_inp, n_tm, scale, x, weights_hbm, table_hbm, held,
    weights, xb, halo, table, low, high, turn, spec, recv, part, got,
    weights_sem, x_sem, table_sem, halo_sem, send_sem, recv_sem, put_sem, got_sem,
):
    me = lax.axis_index("inp")
    seg = lax.axis_index("tm")
    ch_dev, _, _, in_dev, count = recv.shape
    groups, _, _, frame = halo.shape
    rim = halo.shape[1]
    pack = xb.shape[1]
    block = xb.shape[2] - rim
    width = pack * 8
    half = frame // 2
    fold = ch_dev // 2
    inputs = n_inp * in_dev
    rows = inputs // n_tm
    head, per, chunks = plan(ch_dev)
    in_units = in_dev // width
    s_units = count // block
    units = in_units * s_units

    def place(u):
        return lax.rem(u, in_units), lax.rem(u // in_units + 1, s_units)

    def inner_load(u, n):
        g, s = place(u)
        slot = lax.rem(u, 2)
        return pltpu.make_async_copy(
            x.at[g * pack + n, pl.ds(s * block - rim, block + rim)],
            xb.at[slot, n], x_sem.at[slot, n],
        )

    def first_load(u, n):
        g, _ = place(u)
        slot = lax.rem(u, 2)
        return pltpu.make_async_copy(
            x.at[g * pack + n, pl.ds(0, block)],
            xb.at[slot, n, pl.ds(rim, block)], x_sem.at[slot, n],
        )

    def load(u, n, act):
        _, s = place(u)

        @pl.when(s > 0)
        def _():
            act(inner_load(u, n))

        @pl.when(s == 0)
        def _():
            act(first_load(u, n))

    def load_all(u):
        for n in range(pack):
            load(u, n, lambda copy: copy.start())

    def rim_copy():
        return pltpu.make_async_remote_copy(
            src_ref=x.at[:, pl.ds(count - rim, rim)],
            dst_ref=halo,
            send_sem=halo_sem.at[0],
            recv_sem=halo_sem.at[1],
            device_id={"tm": lax.rem(seg + 1, n_tm)},
            device_id_type=MESH,
        )

    weights_copy = pltpu.make_async_copy(weights_hbm, weights, weights_sem.at[0])
    weights_copy.start()
    load_all(0)
    barrier = pltpu.get_barrier_semaphore()
    for d in range(1, n_inp):
        pl.semaphore_signal(
            barrier, inc=1, device_id={"inp": lax.rem(me + d, n_inp)}, device_id_type=MESH
        )
    for d in range(1, n_tm):
        pl.semaphore_signal(
            barrier, inc=1, device_id={"tm": lax.rem(seg + d, n_tm)}, device_id_type=MESH
        )

    table_copy = pltpu.make_async_copy(table_hbm, table, table_sem.at[0])
    table_copy.start()

    def own_head():
        return pltpu.make_async_copy(
            spec.at[me, pl.ds(0, head)], recv.at[pl.ds(0, head), :, me], recv_sem.at[0]
        )

    def channels(c):
        return pl.ds(head + (c - 1) * per, per)

    def own_copy(c):
        return pltpu.make_async_copy(
            spec.at[me, channels(c)], recv.at[channels(c), :, me], recv_sem.at[c]
        )

    def remote(mask, c, src, dst):
        return pltpu.make_async_remote_copy(
            src_ref=src,
            dst_ref=dst,
            send_sem=send_sem.at[0],
            recv_sem=recv_sem.at[c],
            device_id={"inp": across(me, mask, n_inp)[0]},
            device_id_type=MESH,
        )

    def unit_copy(u, mask):
        g, s = place(u)
        peer = across(me, mask, n_inp)[0]
        at = pl.ds(pl.multiple_of(g * width, width), width)
        span = pl.ds(pl.multiple_of(s * block, block), block)
        first = pl.ds(0, head)
        return remote(
            mask, 0, spec.at[peer, first, :, at, span], recv.at[first, :, me, at, span]
        )

    def take(c, chunk):
        pltpu.make_async_copy(recv.at[chunk], recv.at[chunk], recv_sem.at[c]).wait()

    def sent():
        most = spec.at[pl.ds(0, n_inp - 1)]
        pltpu.make_async_copy(most, most, send_sem.at[0]).wait()

    def chunk_copy(c, mask):
        peer = across(me, mask, n_inp)[0]
        return remote(mask, c, spec.at[peer, channels(c)], recv.at[channels(c), :, me])

    def order(k):
        if n_inp & (n_inp - 1) or n_inp < 4:
            return n_inp - 1 - k
        lot = n_inp // 4
        far = n_inp - 1 - 2 * lax.rem(k, lot) - lax.rem(k // lot + me, 2)
        return jnp.where(k < 2 * lot, far, n_inp - 1 - k)

    def send(c):
        own_copy(c).start()
        each(0, n_inp - 1, lambda k: chunk_copy(c, order(k)).start())

    def filter_unit(u):
        slot = lax.rem(u, 2)
        step = 8

        def some(g, k):
            s = k * step
            to = pl.ds(pl.multiple_of((g * block + s) * 8, step * 8), step * 8)
            for t in range(half // LANES):
                sides = []
                for first in (t * LANES, half + t * LANES):
                    lane = slice(first, first + LANES)
                    frames = xb[slot, g, pl.ds(s, step + rim), :, lane].astype(jnp.float32)
                    total = weights[0:1, lane][None] * frames[0:step]
                    for tap in range(1, rim + 1):
                        total = total + weights[tap : tap + 1, lane][None] * frames[tap : tap + step]
                    sides.append(total.reshape(step * 8, LANES))
                low[t, to] = sides[0] + sides[1]
                high[t, to] = sides[0] - sides[1]

        for g in range(pack):
            load(u, g, lambda copy: copy.wait())
            each(0, block // step, functools.partial(some, g))

    def transform(folded, odd, start, size):
        def pair(k):
            two = []
            for i in (2 * k, 2 * k + 1):
                at = (i // 8) * (block * 8) + lax.rem(i, 8)
                two.append(
                    jnp.concatenate(
                        [folded[t, pl.ds(at, block, stride=8), :] for t in range(half // LANES)],
                        axis=1,
                    )
                )
            value = jnp.concatenate(two, axis=0)
            top = value.astype(jnp.bfloat16)
            rest = (value - top.astype(jnp.float32)).astype(jnp.bfloat16)
            side = lax.dot_general(
                table[odd, start : start + size],
                jnp.concatenate([top, top, rest], axis=1),
                (((1,), (1,)), ((), ())),
                preferred_element_type=jnp.float32,
            )
            for n in range(2):
                at = pl.ds(start * width + 2 * k + n, size, stride=width)
                turn[at, :] = side[:, n * block : (n + 1) * block]

        def several(k):
            for n in range(together):
                pair(together * k + n)

        pairs = width // 2
        together = math.gcd(pairs, 8)
        each(0, pairs // together, several)

    def spread(u, odd, start, size):
        g, s = place(u)
        at = pl.ds(pl.multiple_of(g * width, width), width)
        span = pl.ds(pl.multiple_of(s * block, block), block)
        lot = size // (2 * n_inp)
        to = pl.ds(odd * fold + start // (2 * n_inp), lot)
        length = lot * 2 * width

        def some(k):
            first = start * width + k * length
            rows_in = turn[pl.ds(pl.multiple_of(first, length), length), :]
            spec[k, to, :, at, span] = rows_in.astype(jnp.bfloat16).reshape(lot, 2, width, block)

        each(0, n_inp, some)

    front = 2 * n_inp * min(head, fold)

    def spread_all(u, odd):
        spread(u, odd, 0, front)
        if front < half:
            spread(u, odd, front, half - front)

    def unit(u):
        @pl.when(u + 1 < units)
        def _():
            load_all(u + 1)

        g, s = place(u)

        @pl.when(s == 0)
        def _():
            @pl.when(jnp.logical_and(seg > 0, u == units - in_units))
            def _():
                rim_copy().wait_recv()

            @pl.when(jnp.logical_and(seg == 0, u == units - in_units))
            def _():
                halo[...] = jnp.zeros_like(halo)

            xb[lax.rem(u, 2), :, 0:rim] = halo[pl.ds(g * pack, pack)]

        @pl.when(u == 0)
        def _():
            weights_copy.wait()

        filter_unit(u)

        @pl.when(u == 0)
        def _():
            table_copy.wait()

        @pl.when(u == 0)
        def _():
            transform(low, 0, 0, front)
            spread(u, 0, 0, front)
            pl.semaphore_wait(barrier, n_inp - 1 + n_tm - 1)

            @pl.when(seg + 1 < n_tm)
            def _():
                rim_copy().start()

        @pl.when(u > 0)
        def _():
            transform(low, 0, 0, half)
            spread_all(u, 0)

        each(0, n_inp - 1, lambda k: unit_copy(u, order(k)).start())

        @pl.when(u == 0)
        def _():
            if front < half:
                transform(low, 0, front, half - front)
                spread(u, 0, front, half - front)

        transform(high, 1, 0, half)
        spread_all(u, 1)

    each(0, units, unit)
    own_head().start()

    @pl.when(seg + 1 < n_tm)
    def _():
        rim_copy().wait_send()

    def sum_copy(g, p, mask):
        peer = across(seg, mask, n_tm)[0]
        return pltpu.make_async_remote_copy(
            src_ref=part.at[lax.rem(g, RING), peer, p],
            dst_ref=got.at[mask - 1, g, p],
            send_sem=put_sem.at[lax.rem(g, RING)],
            recv_sem=got_sem.at[g],
            device_id={"tm": peer},
            device_id_type=MESH,
        )

    def side(ch, p):
        value = recv[ch, p]
        if in_dev % 16 == 0:
            return value.reshape(inputs, count)
        return value.astype(jnp.float32).reshape(inputs, count).astype(jnp.bfloat16)

    def leave(ch, p, d):
        sum_copy(ch, p, n_tm - d).start()

    def correlate(ch):
        real = side(ch, 0)
        imag = side(ch, 1)
        a = jnp.concatenate([real, imag], axis=1)
        b = jnp.concatenate([imag, -real], axis=1)
        for p, left in ((0, a), (1, b)):
            product = lax.dot_general(
                left, a, (((1,), (1,)), ((), ())), preferred_element_type=jnp.float32
            )
            for q in range(n_tm):
                part[lax.rem(ch, RING), q, p] = product[q * rows : (q + 1) * rows]
            each(1, n_tm, functools.partial(leave, ch, p))

    def put(g):
        slot = lax.rem(g, RING)
        summed = part.at[slot, pl.ds(0, n_tm - 1)]
        pltpu.make_async_copy(summed, summed, put_sem.at[slot]).wait()

    def finish(g):
        summed = got.at[:, g]
        pltpu.make_async_copy(summed, summed, got_sem.at[g]).wait()
        ch = lax.rem(g, fold) * 2 + g // fold
        for p in range(2):
            total = part[lax.rem(g, RING), seg, p]
            for d in range(1, n_tm):
                total = total + got[d - 1, g, p]
            total = total * scale
            for t in range(inputs // LANES):
                at = pl.ds(p * ch_dev + ch, rows, stride=2 * ch_dev)
                held[t, at, :] = total[:, t * LANES : (t + 1) * LANES]

    def done(g):
        early = g + 1 - LATE
        late = ch_dev - SOON - 2 * (ch_dev - 1 - g)
        return jnp.maximum(jnp.maximum(early, late), 0)

    def channel(g):
        @pl.when(g >= RING)
        def _():
            put(g - RING)

        correlate(g)

        each(done(g - 1), done(g), finish)

    ring = me // max(n_inp // 4, 1)
    ahead = jnp.where(jnp.logical_and(ring > 0, ring < 3), INNER, OUTER)
    each(1, jnp.minimum(ahead, chunks), send)
    take(0, pl.ds(0, head))
    each(0, head, channel)

    def step(c):
        @pl.when(c + ahead - 1 < chunks)
        def _():
            send(c + ahead - 1)

        take(c, channels(c))
        each(0, per, lambda k: channel(head + (c - 1) * per + k))

    each(1, chunks, step)
    each(done(ch_dev - 1), ch_dev, finish)
    sent()
    each(
        max(ch_dev - RING, 0),
        ch_dev,
        put,
    )


def deliver(held, out, sem):
    tiles, length, _ = held.shape
    piece = length // PIECES
    copies = [
        pltpu.make_async_copy(
            held.at[t, pl.ds(n * piece, piece)],
            out.at[pl.ds(n * piece, piece), pl.ds(t * LANES, LANES)],
            sem.at[t * PIECES + n],
        )
        for n in range(PIECES)
        for t in range(tiles)
    ]
    for copy in copies:
        copy.start()
    for copy in copies:
        copy.wait()


def tables(frame, n_inp, head):
    fold = frame // 2
    columns = np.arange(fold).reshape(n_inp, fold // (2 * n_inp), 2)
    parts = [columns[:, :head].reshape(-1), columns[:, head:].reshape(-1)]
    order = np.concatenate(parts)
    sides = []
    for odd in (0, 1):
        column = np.arange(fold)
        channel = column // 2 * 2 + odd
        phase = np.arange(fold)[:, None] * channel[None, :] % frame
        angle = phase * (2.0 * math.pi / frame)
        whole = np.where(column % 2 == 0, np.cos(angle), -np.sin(angle)) * frame ** (-0.5)
        whole = whole.T[order].astype(np.float32)
        top = whole.astype(jnp.bfloat16)
        rest = (whole - top.astype(np.float32)).astype(jnp.bfloat16)
        sides.append(np.concatenate([top, rest, top], axis=1))
    return np.stack(sides)


def per_device(samples, tap_weights):
    in_dev = samples.shape[0]
    taps, frame = tap_weights.shape
    rim = taps - 1
    count = samples.shape[1] // frame
    n_inp = lax.axis_size("inp")
    n_tm = lax.axis_size("tm")
    ch_dev = frame // 2 // n_inp
    inputs = n_inp * in_dev
    rows = inputs // n_tm
    groups = in_dev // 8
    pack = math.gcd(groups, 2)
    block = LANES
    chunks = plan(ch_dev)[-1]
    scale = 1.0 / math.sqrt(count * n_tm)
    tiles = inputs // LANES
    frames = samples.reshape(groups, 8, count, frame).transpose(0, 2, 1, 3)
    mine = pl.pallas_call(
        functools.partial(correlator, n_inp, n_tm, scale),
        out_shape=pltpu.VMEM((tiles, rows * 2 * ch_dev, LANES), jnp.float32),
        in_specs=[
            pl.BlockSpec(memory_space=pltpu.HBM),
            pl.BlockSpec(memory_space=pltpu.HBM),
            pl.BlockSpec(memory_space=pltpu.HBM),
        ],
        out_specs=pl.BlockSpec(memory_space=pltpu.VMEM),
        scratch_shapes=[
            pltpu.VMEM((taps, frame), jnp.float32),
            pltpu.VMEM((2, pack, block + rim, 8, frame), jnp.bfloat16),
            pltpu.VMEM((groups, rim, 8, frame), jnp.bfloat16),
            pltpu.VMEM((2, frame // 2, 3 * (frame // 2)), jnp.bfloat16),
            pltpu.VMEM((frame // 2 // LANES, pack * block * 8, LANES), jnp.float32),
            pltpu.VMEM((frame // 2 // LANES, pack * block * 8, LANES), jnp.float32),
            pltpu.VMEM((frame // 2 * pack * 8, block), jnp.float32),
            pltpu.VMEM((n_inp, ch_dev, 2, in_dev, count), jnp.bfloat16),
            pltpu.VMEM((ch_dev, 2, n_inp, in_dev, count), jnp.bfloat16),
            pltpu.VMEM((RING, n_tm, 2, rows, inputs), jnp.float32),
            pltpu.VMEM((n_tm - 1, ch_dev, 2, rows, inputs), jnp.float32),
            pltpu.SemaphoreType.DMA((1,)),
            pltpu.SemaphoreType.DMA((2, pack)),
            pltpu.SemaphoreType.DMA((1,)),
            pltpu.SemaphoreType.DMA((2,)),
            pltpu.SemaphoreType.DMA((1,)),
            pltpu.SemaphoreType.DMA((chunks,)),
            pltpu.SemaphoreType.DMA((RING,)),
            pltpu.SemaphoreType.DMA((ch_dev,)),
        ],
        compiler_params=pltpu.CompilerParams(
            collective_id=0, has_side_effects=True, vmem_limit_bytes=58 << 20
        ),
    )(frames, tap_weights, jnp.asarray(tables(frame, n_inp, plan(ch_dev)[0])))
    whole = pl.pallas_call(
        deliver,
        out_shape=jax.ShapeDtypeStruct((rows * 2 * ch_dev, inputs), jnp.float32),
        in_specs=[pl.BlockSpec(memory_space=pltpu.VMEM)],
        out_specs=pl.BlockSpec(memory_space=pltpu.HBM),
        scratch_shapes=[pltpu.SemaphoreType.DMA((tiles * PIECES,))],
        compiler_params=pltpu.CompilerParams(vmem_limit_bytes=8 << 20),
    )(pltpu.with_memory_space_constraint(mine, pltpu.VMEM))
    return whole.reshape(rows, 2, ch_dev, inputs)


def solution(mesh):
    return jax.shard_map(
        per_device,
        mesh=mesh,
        in_specs=(P("inp", "tm"), P()),
        out_specs=P("tm", None, "inp", None),
        check_vma=False,
    )
```

```python
import functools
import math

import jax
import jax.numpy as jnp
import numpy as np
from jax import lax
from jax.experimental import pallas as pl
from jax.experimental.pallas import tpu as pltpu
from jax.sharding import PartitionSpec as P

MESH = pl.DeviceIdType.MESH
HEAD = 4
STEPS = 32
OUTER = 1
INNER = 2
LATE = 8
SOON = 1
RING = 12
LANES = 128
PIECES = 1


def each(first, end, body):
    def step(d, carry):
        body(d)
        return carry

    lax.fori_loop(first, end, step, 0)


def across(me, mask, n):
    if n & (n - 1):
        return lax.rem(me + mask, n), lax.rem(me + n - mask, n)
    peer, bit = me, 1
    while bit < n:
        flip = lax.rem(mask // bit, 2)
        peer = peer + flip * bit * (1 - 2 * lax.rem(me // bit, 2))
        bit *= 2
    return peer, peer


def plan(ch_dev):
    head = max(ch_dev // HEAD, 1)
    per = math.gcd(max(ch_dev // STEPS, 1), ch_dev - head)
    return head, per, 1 + (ch_dev - head) // per


def correlator(
    n_inp, n_tm, scale, x, weights_hbm, table_hbm, held,
    weights, xb, halo, table, low, high, turn, spec, recv, part, got,
    weights_sem, x_sem, table_sem, halo_sem, send_sem, recv_sem, put_sem, got_sem,
):
    me = lax.axis_index("inp")
    seg = lax.axis_index("tm")
    ch_dev, _, _, in_dev, count = recv.shape
    groups, _, _, frame = halo.shape
    rim = halo.shape[1]
    pack = xb.shape[1]
    block = xb.shape[2] - rim
    width = pack * 8
    half = frame // 2
    fold = ch_dev // 2
    inputs = n_inp * in_dev
    rows = inputs // n_tm
    head, per, chunks = plan(ch_dev)
    in_units = in_dev // width
    s_units = count // block
    units = in_units * s_units

    def place(u):
        return lax.rem(u, in_units), lax.rem(u // in_units + 1, s_units)

    def inner_load(u, n):
        g, s = place(u)
        slot = lax.rem(u, 2)
        return pltpu.make_async_copy(
            x.at[g * pack + n, pl.ds(s * block - rim, block + rim)],
            xb.at[slot, n], x_sem.at[slot, n],
        )

    def first_load(u, n):
        g, _ = place(u)
        slot = lax.rem(u, 2)
        return pltpu.make_async_copy(
            x.at[g * pack + n, pl.ds(0, block)],
            xb.at[slot, n, pl.ds(rim, block)], x_sem.at[slot, n],
        )

    def load(u, n, act):
        _, s = place(u)

        @pl.when(s > 0)
        def _():
            act(inner_load(u, n))

        @pl.when(s == 0)
        def _():
            act(first_load(u, n))

    def load_all(u):
        for n in range(pack):
            load(u, n, lambda copy: copy.start())

    def rim_copy():
        return pltpu.make_async_remote_copy(
            src_ref=x.at[:, pl.ds(count - rim, rim)],
            dst_ref=halo,
            send_sem=halo_sem.at[0],
            recv_sem=halo_sem.at[1],
            device_id={"tm": lax.rem(seg + 1, n_tm)},
            device_id_type=MESH,
        )

    weights_copy = pltpu.make_async_copy(weights_hbm, weights, weights_sem.at[0])
    weights_copy.start()
    load_all(0)
    barrier = pltpu.get_barrier_semaphore()
    for d in range(1, n_inp):
        pl.semaphore_signal(
            barrier, inc=1, device_id={"inp": lax.rem(me + d, n_inp)}, device_id_type=MESH
        )
    for d in range(1, n_tm):
        pl.semaphore_signal(
            barrier, inc=1, device_id={"tm": lax.rem(seg + d, n_tm)}, device_id_type=MESH
        )

    table_copy = pltpu.make_async_copy(table_hbm, table, table_sem.at[0])
    table_copy.start()

    def own_head():
        return pltpu.make_async_copy(
            spec.at[me, pl.ds(0, head)], recv.at[pl.ds(0, head), :, me], recv_sem.at[0]
        )

    def channels(c):
        return pl.ds(head + (c - 1) * per, per)

    def own_copy(c):
        return pltpu.make_async_copy(
            spec.at[me, channels(c)], recv.at[channels(c), :, me], recv_sem.at[c]
        )

    def remote(mask, c, src, dst):
        return pltpu.make_async_remote_copy(
            src_ref=src,
            dst_ref=dst,
            send_sem=send_sem.at[0],
            recv_sem=recv_sem.at[c],
            device_id={"inp": across(me, mask, n_inp)[0]},
            device_id_type=MESH,
        )

    def unit_copy(u, mask):
        g, s = place(u)
        peer = across(me, mask, n_inp)[0]
        at = pl.ds(pl.multiple_of(g * width, width), width)
        span = pl.ds(pl.multiple_of(s * block, block), block)
        first = pl.ds(0, head)
        return remote(
            mask, 0, spec.at[peer, first, :, at, span], recv.at[first, :, me, at, span]
        )

    def take(c, chunk):
        pltpu.make_async_copy(recv.at[chunk], recv.at[chunk], recv_sem.at[c]).wait()

    def sent():
        most = spec.at[pl.ds(0, n_inp - 1)]
        pltpu.make_async_copy(most, most, send_sem.at[0]).wait()

    def chunk_copy(c, mask):
        peer = across(me, mask, n_inp)[0]
        return remote(mask, c, spec.at[peer, channels(c)], recv.at[channels(c), :, me])

    def order(k):
        if n_inp & (n_inp - 1) or n_inp < 4:
            return n_inp - 1 - k
        lot = n_inp // 4
        far = n_inp - 1 - 2 * lax.rem(k, lot) - lax.rem(k // lot + me, 2)
        return jnp.where(k < 2 * lot, far, n_inp - 1 - k)

    def send(c):
        own_copy(c).start()
        each(0, n_inp - 1, lambda k: chunk_copy(c, order(k)).start())

    def filter_unit(u):
        slot = lax.rem(u, 2)
        step = 8

        def some(g, k):
            s = k * step
            to = pl.ds(pl.multiple_of((g * block + s) * 8, step * 8), step * 8)
            for t in range(half // LANES):
                sides = []
                for first in (t * LANES, half + t * LANES):
                    lane = slice(first, first + LANES)
                    frames = xb[slot, g, pl.ds(s, step + rim), :, lane].astype(jnp.float32)
                    total = weights[0:1, lane][None] * frames[0:step]
                    for tap in range(1, rim + 1):
                        total = total + weights[tap : tap + 1, lane][None] * frames[tap : tap + step]
                    sides.append(total.reshape(step * 8, LANES))
                low[t, to] = sides[0] + sides[1]
                high[t, to] = sides[0] - sides[1]

        for g in range(pack):
            load(u, g, lambda copy: copy.wait())
            each(0, block // step, functools.partial(some, g))

    def transform(folded, odd, start, size):
        def pair(k):
            two = []
            for i in (2 * k, 2 * k + 1):
                at = (i // 8) * (block * 8) + lax.rem(i, 8)
                two.append(
                    jnp.concatenate(
                        [folded[t, pl.ds(at, block, stride=8), :] for t in range(half // LANES)],
                        axis=1,
                    )
                )
            value = jnp.concatenate(two, axis=0)
            top = value.astype(jnp.bfloat16)
            rest = (value - top.astype(jnp.float32)).astype(jnp.bfloat16)
            side = lax.dot_general(
                table[odd, start : start + size],
                jnp.concatenate([top, top, rest], axis=1),
                (((1,), (1,)), ((), ())),
                preferred_element_type=jnp.float32,
            )
            for n in range(2):
                at = pl.ds(start * width + 2 * k + n, size, stride=width)
                turn[at, :] = side[:, n * block : (n + 1) * block]

        def several(k):
            for n in range(together):
                pair(together * k + n)

        pairs = width // 2
        together = math.gcd(pairs, 8)
        each(0, pairs // together, several)

    def spread(u, odd, start, size):
        g, s = place(u)
        at = pl.ds(pl.multiple_of(g * width, width), width)
        span = pl.ds(pl.multiple_of(s * block, block), block)
        lot = size // (2 * n_inp)
        to = pl.ds(odd * fold + start // (2 * n_inp), lot)
        length = lot * 2 * width

        def some(k):
            first = start * width + k * length
            rows_in = turn[pl.ds(pl.multiple_of(first, length), length), :]
            spec[k, to, :, at, span] = rows_in.astype(jnp.bfloat16).reshape(lot, 2, width, block)

        each(0, n_inp, some)

    front = 2 * n_inp * min(head, fold)

    def spread_all(u, odd):
        spread(u, odd, 0, front)
        if front < half:
            spread(u, odd, front, half - front)

    def unit(u):
        @pl.when(u + 1 < units)
        def _():
            load_all(u + 1)

        g, s = place(u)

        @pl.when(s == 0)
        def _():
            @pl.when(jnp.logical_and(seg > 0, u == units - in_units))
            def _():
                rim_copy().wait_recv()

            @pl.when(jnp.logical_and(seg == 0, u == units - in_units))
            def _():
                halo[...] = jnp.zeros_like(halo)

            xb[lax.rem(u, 2), :, 0:rim] = halo[pl.ds(g * pack, pack)]

        @pl.when(u == 0)
        def _():
            weights_copy.wait()

        filter_unit(u)

        @pl.when(u == 0)
        def _():
            table_copy.wait()

        @pl.when(u == 0)
        def _():
            transform(low, 0, 0, front)
            spread(u, 0, 0, front)
            pl.semaphore_wait(barrier, n_inp - 1 + n_tm - 1)

            @pl.when(seg + 1 < n_tm)
            def _():
                rim_copy().start()

        @pl.when(u > 0)
        def _():
            transform(low, 0, 0, half)
            spread_all(u, 0)

        each(0, n_inp - 1, lambda k: unit_copy(u, order(k)).start())

        @pl.when(u == 0)
        def _():
            if front < half:
                transform(low, 0, front, half - front)
                spread(u, 0, front, half - front)

        transform(high, 1, 0, half)
        spread_all(u, 1)

    each(0, units, unit)
    own_head().start()

    @pl.when(seg + 1 < n_tm)
    def _():
        rim_copy().wait_send()

    def sum_copy(g, p, mask):
        peer = across(seg, mask, n_tm)[0]
        return pltpu.make_async_remote_copy(
            src_ref=part.at[lax.rem(g, RING), peer, p],
            dst_ref=got.at[mask - 1, g, p],
            send_sem=put_sem.at[lax.rem(g, RING)],
            recv_sem=got_sem.at[g],
            device_id={"tm": peer},
            device_id_type=MESH,
        )

    def side(ch, p):
        value = recv[ch, p]
        if in_dev % 16 == 0:
            return value.reshape(inputs, count)
        return value.astype(jnp.float32).reshape(inputs, count).astype(jnp.bfloat16)

    def leave(ch, p, d):
        sum_copy(ch, p, n_tm - d).start()

    def correlate(ch):
        real = side(ch, 0)
        imag = side(ch, 1)
        a = jnp.concatenate([real, imag], axis=1)
        b = jnp.concatenate([imag, -real], axis=1)
        for p, left in ((0, a), (1, b)):
            product = lax.dot_general(
                left, a, (((1,), (1,)), ((), ())), preferred_element_type=jnp.float32
            )
            for q in range(n_tm):
                part[lax.rem(ch, RING), q, p] = product[q * rows : (q + 1) * rows]
            each(1, n_tm, functools.partial(leave, ch, p))

    def put(g):
        slot = lax.rem(g, RING)
        summed = part.at[slot, pl.ds(0, n_tm - 1)]
        pltpu.make_async_copy(summed, summed, put_sem.at[slot]).wait()

    def finish(g):
        summed = got.at[:, g]
        pltpu.make_async_copy(summed, summed, got_sem.at[g]).wait()
        ch = lax.rem(g, fold) * 2 + g // fold
        for p in range(2):
            total = part[lax.rem(g, RING), seg, p]
            for d in range(1, n_tm):
                total = total + got[d - 1, g, p]
            total = total * scale
            for t in range(inputs // LANES):
                at = pl.ds(p * ch_dev + ch, rows, stride=2 * ch_dev)
                held[t, at, :] = total[:, t * LANES : (t + 1) * LANES]

    def done(g):
        early = g + 1 - LATE
        late = ch_dev - SOON - 2 * (ch_dev - 1 - g)
        return jnp.maximum(jnp.maximum(early, late), 0)

    def channel(g):
        @pl.when(g >= RING)
        def _():
            put(g - RING)

        correlate(g)

        each(done(g - 1), done(g), finish)

    ring = me // max(n_inp // 4, 1)
    ahead = jnp.where(jnp.logical_and(ring > 0, ring < 3), INNER, OUTER)
    each(1, jnp.minimum(ahead, chunks), send)
    take(0, pl.ds(0, head))
    each(0, head, channel)

    def step(c):
        @pl.when(c + ahead - 1 < chunks)
        def _():
            send(c + ahead - 1)

        take(c, channels(c))
        each(0, per, lambda k: channel(head + (c - 1) * per + k))

    each(1, chunks, step)
    each(done(ch_dev - 1), ch_dev, finish)
    sent()
    each(
        max(ch_dev - RING, 0),
        ch_dev,
        put,
    )


def deliver(held, out, sem):
    tiles, length, _ = held.shape
    piece = length // PIECES
    copies = [
        pltpu.make_async_copy(
            held.at[t, pl.ds(n * piece, piece)],
            out.at[pl.ds(n * piece, piece), pl.ds(t * LANES, LANES)],
            sem.at[t * PIECES + n],
        )
        for n in range(PIECES)
        for t in range(tiles)
    ]
    for copy in copies:
        copy.start()
    for copy in copies:
        copy.wait()


def tables(frame, n_inp, head):
    fold = frame // 2
    columns = np.arange(fold).reshape(n_inp, fold // (2 * n_inp), 2)
    parts = [columns[:, :head].reshape(-1), columns[:, head:].reshape(-1)]
    order = np.concatenate(parts)
    sides = []
    for odd in (0, 1):
        column = np.arange(fold)
        channel = column // 2 * 2 + odd
        phase = np.arange(fold)[:, None] * channel[None, :] % frame
        angle = phase * (2.0 * math.pi / frame)
        whole = np.where(column % 2 == 0, np.cos(angle), -np.sin(angle)) * frame ** (-0.5)
        whole = whole.T[order].astype(np.float32)
        top = whole.astype(jnp.bfloat16)
        rest = (whole - top.astype(np.float32)).astype(jnp.bfloat16)
        sides.append(np.concatenate([top, rest, top], axis=1))
    return np.stack(sides)


def per_device(samples, tap_weights):
    in_dev = samples.shape[0]
    taps, frame = tap_weights.shape
    rim = taps - 1
    count = samples.shape[1] // frame
    n_inp = lax.axis_size("inp")
    n_tm = lax.axis_size("tm")
    ch_dev = frame // 2 // n_inp
    inputs = n_inp * in_dev
    rows = inputs // n_tm
    groups = in_dev // 8
    pack = math.gcd(groups, 2)
    block = LANES
    chunks = plan(ch_dev)[-1]
    scale = 1.0 / math.sqrt(count * n_tm)
    tiles = inputs // LANES
    frames = samples.reshape(groups, 8, count, frame).transpose(0, 2, 1, 3)
    mine = pl.pallas_call(
        functools.partial(correlator, n_inp, n_tm, scale),
        out_shape=pltpu.VMEM((tiles, rows * 2 * ch_dev, LANES), jnp.float32),
        in_specs=[
            pl.BlockSpec(memory_space=pltpu.HBM),
            pl.BlockSpec(memory_space=pltpu.HBM),
            pl.BlockSpec(memory_space=pltpu.HBM),
        ],
        out_specs=pl.BlockSpec(memory_space=pltpu.VMEM),
        scratch_shapes=[
            pltpu.VMEM((taps, frame), jnp.float32),
            pltpu.VMEM((2, pack, block + rim, 8, frame), jnp.bfloat16),
            pltpu.VMEM((groups, rim, 8, frame), jnp.bfloat16),
            pltpu.VMEM((2, frame // 2, 3 * (frame // 2)), jnp.bfloat16),
            pltpu.VMEM((frame // 2 // LANES, pack * block * 8, LANES), jnp.float32),
            pltpu.VMEM((frame // 2 // LANES, pack * block * 8, LANES), jnp.float32),
            pltpu.VMEM((frame // 2 * pack * 8, block), jnp.float32),
            pltpu.VMEM((n_inp, ch_dev, 2, in_dev, count), jnp.bfloat16),
            pltpu.VMEM((ch_dev, 2, n_inp, in_dev, count), jnp.bfloat16),
            pltpu.VMEM((RING, n_tm, 2, rows, inputs), jnp.float32),
            pltpu.VMEM((n_tm - 1, ch_dev, 2, rows, inputs), jnp.float32),
            pltpu.SemaphoreType.DMA((1,)),
            pltpu.SemaphoreType.DMA((2, pack)),
            pltpu.SemaphoreType.DMA((1,)),
            pltpu.SemaphoreType.DMA((2,)),
            pltpu.SemaphoreType.DMA((1,)),
            pltpu.SemaphoreType.DMA((chunks,)),
            pltpu.SemaphoreType.DMA((RING,)),
            pltpu.SemaphoreType.DMA((ch_dev,)),
        ],
        compiler_params=pltpu.CompilerParams(
            collective_id=0, has_side_effects=True, vmem_limit_bytes=58 << 20
        ),
    )(frames, tap_weights, jnp.asarray(tables(frame, n_inp, plan(ch_dev)[0])))
    whole = pl.pallas_call(
        deliver,
        out_shape=jax.ShapeDtypeStruct((rows * 2 * ch_dev, inputs), jnp.float32),
        in_specs=[pl.BlockSpec(memory_space=pltpu.VMEM)],
        out_specs=pl.BlockSpec(memory_space=pltpu.HBM),
        scratch_shapes=[pltpu.SemaphoreType.DMA((tiles * PIECES,))],
        compiler_params=pltpu.CompilerParams(vmem_limit_bytes=8 << 20),
    )(pltpu.with_memory_space_constraint(mine, pltpu.VMEM))
    return whole.reshape(rows, 2, ch_dev, inputs)


def solution(mesh):
    return jax.shard_map(
        per_device,
        mesh=mesh,
        in_specs=(P("inp", "tm"), P()),
        out_specs=P("tm", None, "inp", None),
        check_vma=False,
    )
```
